256 devices in a mesh: seq: 64 (over x, z, y_hi), tp: 4 (over y_lo, core).
Axes of the slice: x: 4, y: 4 (y_hi: 2, y_lo: 2; y = y_hi * 2 + y_lo), z: 8, core: 2. Of those that a mesh axis runs over, the one named last changes fastest.
Arguments:
- tree_hidden: bfloat16 [128, 8192], P(None, 'seq'), may hold values from -6 to 6
- query_low: bfloat16 [128, 8192], P('seq', 'tp'), may hold values from -24 to 24
- key_tree_low: bfloat16 [128, 1024], P('seq', 'tp'), may hold values from -20 to 20
- value_tree_low: bfloat16 [128, 1024], P('seq', 'tp'), may hold values from -6 to 6
- cache_keys: bfloat16 [8, 65536, 8, 128], P(None, 'seq', 'tp'), may hold values from -40 to 40
- cache_values: bfloat16 [8, 65536, 8, 128], P(None, 'seq', 'tp'), may hold values from -6 to 6
- cache_lengths: int32 [8], replicated, may hold values from 8192 to 65536
- ancestors: int32 [8, 16, 16], replicated, may hold values from 0 to 1, as said below
- out_weight: bfloat16 [8192, 8192], P('tp', 'seq'), may hold values from -0.0625 to 0.0625
- norm_gain: float32 [8192], P('seq'), may hold values from 0.1 to 1.9
- w_query_up: bfloat16 [8192, 8192], P('seq', 'tp'), may hold values from -0.0625 to 0.0625
- w_key_up: bfloat16 [8192, 1024], P('seq', 'tp'), may hold values from -0.5 to 0.5
- w_value_up: bfloat16 [8192, 1024], P('seq', 'tp'), may hold values from -0.0625 to 0.0625
- retained_keys: bfloat16 [64, 512, 8, 128], P('seq', None, 'tp'), may hold values from -400 to 400
- retained_values: bfloat16 [64, 512, 8, 128], P('seq', None, 'tp'), may hold values from -6 to 6
- retained_index: int32 [64, 512, 8], P('seq', None, 'tp'), may hold values from 0 to 65535
Outputs:
- residual: float32 [128, 8192], P(None, 'seq')
- upper_heads: float32 [128, 8192], P('seq', 'tp')
The draws below stay inside these ranges and needn't reach their ends.
Inputs may be any that keep to these rules, and one draw needn't show every extreme that they name: ancestors[r, i, j] is 1 when node j is node i or an ancestor of node i in request r's tree, else 0; node 0 is the root and every other node's parent has a lower number.
All inputs are finite; a program needn't handle non-finite values.
Results may differ from the reference program's by a relative error of at most 0.04.
Values may be sent and summed in bfloat16 or wider, within the bound.
No kernel may reach another device: no remote copies, remote signals or barrier semaphores. Data moves between devices by JAX's collectives and lax.ppermute only.
A program may use at most 64 MiB of HBM per device.

```python
import jax
import jax.numpy as jnp
from jax import lax

D = 8192
HQ = 64
KVH = 8
HD = 128
NODES = 16
GROUP = 8
RET = 4096
R = 8
M = 128
CACHE = 65536
RET_PART = 512


def tree_queries(key):
    drawn = jax.random.normal(jax.random.fold_in(key, 101), (R * NODES, HQ * HD), jnp.float32) * 4.0
    return jnp.clip(drawn, -24.0, 24.0)


def draw_query_low(key, part):
    return tree_queries(key).astype(jnp.bfloat16)


def draw_cache_keys(key, part):
    array_shape = (R, CACHE, KVH, HD)
    key_rows = jnp.clip(jax.random.normal(jax.random.fold_in(key, 103), array_shape, jnp.float32), -5.0, 5.0)
    return key_rows.astype(jnp.bfloat16)


def draw_retained_keys(key, part):
    array_shape = (R * GROUP, RET // GROUP, KVH, HD)
    key_rows = jnp.clip(jax.random.normal(jax.random.fold_in(key, 106), array_shape, jnp.float32) * 4.0, -24.0, 24.0)
    return key_rows.astype(jnp.bfloat16)


def draw_ancestors(key, part):
    random_bits = jax.random.randint(jax.random.fold_in(key, 107), (R, NODES), 0, 1 << 20)
    node_ids = jnp.arange(NODES, dtype=jnp.int32)
    parent_span = jnp.minimum(jnp.maximum(node_ids, 1), 8)
    parents = jnp.maximum(node_ids[None, :] - 1 - random_bits % parent_span[None, :], 0)
    identity = (node_ids[:, None] == node_ids[None, :]).astype(jnp.int32)
    ancestry = jnp.broadcast_to(identity, (R, NODES, NODES))
    request_ids = jnp.arange(R, dtype=jnp.int32)

    def extend(node_index, table):
        parent_row = table[request_ids, parents[:, node_index]]
        new_row = jnp.maximum(parent_row, (node_ids == node_index).astype(jnp.int32)[None, :])
        return table.at[:, node_index].set(new_row)
    return lax.fori_loop(1, NODES, extend, ancestry)


def set_ends(result, rng, least, largest):
    place = [jax.random.randint(jax.random.fold_in(rng, axis), (), 0, length) for axis, length in enumerate(result.shape)]
    widest = result.shape.index(max(result.shape))
    neighbour = place[:widest] + [(place[widest] + 1) % result.shape[widest]] + place[widest + 1:]
    return result.at[tuple(place)].set(least).at[tuple(neighbour)].set(largest)


def levels(rng, extent, pieces, low, top_value):
    gain = 1.0
    for dim, blocks in pieces:
        heights = jax.random.uniform(jax.random.fold_in(jax.random.fold_in(rng, 6), dim), (blocks,), jnp.float32, low / len(pieces), top_value / len(pieces))
        gain = gain * jnp.repeat(jnp.exp(heights), extent[dim] // blocks).reshape((-1,) + (1,) * (len(extent) - 1 - dim))
    return gain


def normal_values(rng, shape, width, reach, split=(), kind=jnp.bfloat16):
    loudness = levels(rng, shape, split, -0.22, 0.18) if split else 1.0
    values = jax.random.normal(rng, shape, jnp.float32) * width * loudness
    return jnp.minimum(jnp.maximum(values, -reach), reach).astype(kind)


def setup_inputs(seed: int = 0) -> dict:
    key_list = jax.random.split(jax.random.key(seed), 17)
    return {
        "tree_hidden": normal_values(key_list[0], (M, D), 1.0, 6.0, ((1, 64),)),
        "query_low": draw_query_low(jax.random.fold_in(key_list[16], 71), 0),
        "key_tree_low": normal_values(key_list[2], (M, KVH * HD), 3.5, 20.0, ((0, 64), (1, 4))),
        "value_tree_low": normal_values(key_list[3], (M, KVH * HD), 1.0, 6.0, ((0, 64), (1, 4))),
        "cache_keys": draw_cache_keys(jax.random.fold_in(key_list[16], 71), 0),
        "cache_values": normal_values(key_list[5], (R, CACHE, KVH, HD), 1.0, 6.0, ((1, 64), (2, 4))),
        "cache_lengths": set_ends(jax.random.randint(key_list[6], (R,), CACHE // 8, CACHE + 1), jax.random.fold_in(key_list[6], 1), CACHE // 8, CACHE).astype(jnp.int32),
        "ancestors": draw_ancestors(jax.random.fold_in(key_list[16], 71), 0),
        "out_weight": normal_values(key_list[8], (HQ * HD, D), (HQ * HD) ** -0.5, 0.0625, ((0, 4), (1, 64))),
        "norm_gain": jnp.clip(1.0 + 0.18 * jax.random.normal(key_list[9], (D,), jnp.float32), 0.1, 1.9),
        "w_query_up": normal_values(key_list[10], (D, HQ * HD), D ** -0.5, 0.0625, ((0, 64), (1, 4))),
        "w_key_up": normal_values(key_list[11], (D, KVH * HD), (D // 64) ** -0.5, 0.5, ((0, 64), (1, 4))),
        "w_value_up": normal_values(key_list[12], (D, KVH * HD), D ** -0.5, 0.0625, ((0, 64), (1, 4))),
        "retained_keys": draw_retained_keys(jax.random.fold_in(key_list[16], 71), 0),
        "retained_values": normal_values(key_list[14], (R * GROUP, RET_PART, KVH, HD), 1.0, 6.0, ((0, 64), (2, 4))),
        "retained_index": set_ends(jax.random.randint(key_list[15], (R * GROUP, RET_PART, KVH), 0, CACHE), jax.random.fold_in(key_list[15], 1), 0, CACHE - 1).astype(jnp.int32),
    }


masked_score = -1e+30
norm_epsilon = 1e-05

def joint_attend(query_rows, far_keys, far_values, far_allowed, near_keys, near_values, near_mask):
    row_count = query_rows.shape[0]
    group_size = HQ // KVH
    queries = query_rows.astype(jnp.float32).reshape(row_count, KVH, group_size, HD).transpose(1, 0, 2, 3)
    near_key_rows = near_keys.astype(jnp.float32).reshape(-1, KVH, HD).transpose(1, 0, 2)
    near_value_rows = near_values.astype(jnp.float32).reshape(-1, KVH, HD).transpose(1, 0, 2)
    near_usable = near_mask > 0

    def one_head(operands):
        head_query, key_rows, value_rows, usable, tree_keys, tree_values = operands
        far_scores = jnp.einsum('ngd,cd->ngc', head_query, key_rows.astype(jnp.float32)) * HD ** (-0.5)
        near_scores = jnp.einsum('ngd,md->ngm', head_query, tree_keys) * HD ** (-0.5)
        scores = jnp.concatenate([far_scores, near_scores], axis=-1)
        allowed = jnp.concatenate([jnp.broadcast_to(usable[None, None, :], far_scores.shape), jnp.broadcast_to(near_usable[:, None, :], near_scores.shape)], axis=-1)
        masked = jnp.where(allowed, scores, masked_score)
        highest = lax.optimization_barrier(jnp.max(masked, axis=-1, keepdims=True))
        weights = jnp.where(allowed, jnp.exp(masked - highest), 0.0)
        weight_sum = lax.optimization_barrier(jnp.sum(weights, axis=-1, keepdims=True))
        rounded = lax.optimization_barrier(weights.astype(jnp.bfloat16)).astype(jnp.float32)
        both_values = jnp.concatenate([value_rows.astype(jnp.float32), tree_values], axis=0)
        return jnp.einsum('ngc,cd->ngd', rounded, both_values) / weight_sum
    blended = lax.map(one_head, (queries, far_keys.transpose(1, 0, 2), far_values.transpose(1, 0, 2), far_allowed.T, near_key_rows, near_value_rows))
    return blended.transpose(1, 0, 2, 3).reshape(row_count, HQ * HD).astype(jnp.float32)

def reference(tree_hidden, query_low, key_tree_low, value_tree_low, cache_keys, cache_values, cache_lengths, ancestors, out_weight, norm_gain, w_query_up, w_key_up, w_value_up, retained_keys, retained_values, retained_index):
    positions = jnp.arange(CACHE, dtype=jnp.int32)

    def lower_request(operands):
        query_rows, key_rows, value_rows, seq_length, tree_keys, tree_values, tree_mask = operands
        usable = jnp.broadcast_to((positions < seq_length)[:, None], (CACHE, KVH))
        return joint_attend(query_rows, key_rows, value_rows, usable, tree_keys, tree_values, tree_mask).astype(jnp.bfloat16)
    lower = lax.map(lower_request, (query_low.reshape(R, NODES, HQ * HD), cache_keys, cache_values, cache_lengths, key_tree_low.reshape(R, NODES, KVH * HD), value_tree_low.reshape(R, NODES, KVH * HD), ancestors)).reshape(R * NODES, HQ * HD)
    summed = jnp.dot(lower, out_weight, preferred_element_type=jnp.float32)
    residual = tree_hidden.astype(jnp.float32) + summed
    inverse = lax.rsqrt(lax.optimization_barrier(jnp.mean(residual * residual, axis=1, keepdims=True)) + norm_epsilon)
    normed = (residual * inverse * norm_gain[None, :]).astype(jnp.bfloat16)
    query_up = jnp.dot(normed, w_query_up, preferred_element_type=jnp.float32).astype(jnp.bfloat16)
    key_up = jnp.dot(normed, w_key_up, preferred_element_type=jnp.float32).astype(jnp.bfloat16)
    value_up = jnp.dot(normed, w_value_up, preferred_element_type=jnp.float32).astype(jnp.bfloat16)

    def upper_request(operands):
        query_rows, key_rows, value_rows, positions_kept, seq_length, tree_keys, tree_values, tree_mask = operands
        return joint_attend(query_rows, key_rows, value_rows, positions_kept < seq_length, tree_keys, tree_values, tree_mask)
    upper = lax.map(upper_request, (query_up.reshape(R, NODES, HQ * HD), retained_keys.reshape(R, RET, KVH, HD), retained_values.reshape(R, RET, KVH, HD), retained_index.reshape(R, RET, KVH), cache_lengths, key_up.reshape(R, NODES, KVH * HD), value_up.reshape(R, NODES, KVH * HD), ancestors)).reshape(R * NODES, HQ * HD)
    return (residual, upper)
```

```python
import functools

import jax
import jax.numpy as jnp
from jax import lax
from jax.experimental import pallas as pl
from jax.experimental.pallas import tpu as pltpu
from jax.sharding import Mesh, PartitionSpec as P

HD = 128
GROUP = 8
SCALE = HD ** (-0.5)
SCALE2 = SCALE * 1.4426950408889634
MASKED = -1e30
FLOOR = -1e20
EPS = 1e-05
F32 = jnp.float32
BF16 = jnp.bfloat16

SEQ = ("x", "zh", "zl", "yh")
TEAM = ("zl", "yh")


def contract(a, b, dims):
    return lax.dot_general(a, b, (dims, ((), ())), preferred_element_type=F32)


def exchanged(blocks, axis):
    return lax.all_to_all(blocks, axis, split_axis=0, concat_axis=0, tiled=True)


def spread(array, axis):
    copies = jnp.broadcast_to(array, (lax.axis_size(axis), *array.shape))
    return exchanged(copies, axis)


def head_halves(rows):
    parity = lax.broadcasted_iota(jnp.int32, (16, HD), 0) % 2
    even = (parity == 0).astype(F32).astype(BF16)
    odd = (parity == 1).astype(F32).astype(BF16)
    count = rows.shape[0] // 16
    tiles = rows.reshape(count, 16, HD)
    first = (tiles * even[None]).reshape(rows.shape)
    second = (tiles * odd[None]).reshape(rows.shape)
    return jnp.concatenate([first, second], axis=1)


def pair_max(scores):
    width = scores.shape[1]
    folded = scores[:, 0:HD]
    for c in range(HD, width, HD):
        folded = jnp.maximum(folded, scores[:, c : c + HD])
    odd = lax.broadcasted_iota(jnp.int32, folded.shape, 1) % 2 == 1
    m0 = jnp.max(jnp.where(odd, MASKED, folded), axis=1, keepdims=True)
    m1 = jnp.max(jnp.where(odd, folded, MASKED), axis=1, keepdims=True)
    return m0, m1, odd


def shift_of(maximum):
    return jnp.maximum(maximum, FLOOR).astype(BF16).astype(F32)


def pair_weights(scores, s0, s1, odd):
    width = scores.shape[1]
    shift = jnp.where(odd, s1, s0)
    pieces = []
    total = jnp.zeros((scores.shape[0], HD), F32)
    for c in range(0, width, HD):
        w = jnp.exp2(scores[:, c : c + HD] - shift)
        total = total + w
        pieces.append(w.astype(BF16))
    l0 = jnp.sum(jnp.where(odd, 0.0, total), axis=1, keepdims=True)
    l1 = jnp.sum(jnp.where(odd, total, 0.0), axis=1, keepdims=True)
    return jnp.concatenate(pieces, axis=1), l0, l1


def stat_tile(s0, s1, l0, l1):
    lane = lax.broadcasted_iota(jnp.int32, (s0.shape[0], HD), 1)
    return jnp.where(
        lane < 64, jnp.where(lane < 32, s0, s1), jnp.where(lane < 96, l0, l1)
    )


def turn_kernel(k_hbm, kt_ref, k_buf, sems):
    requests, keys, _ = k_buf.shape
    step = 256

    def copy(r):
        return pltpu.make_async_copy(k_hbm.at[r], k_buf.at[r], sems.at[r])

    for r in range(requests):
        copy(r).start()
    for r in range(requests):
        copy(r).wait()
        for c in range(0, keys, step):
            kt_ref[r, :, c : c + step] = k_buf[r, c : c + step, :].T


def turn(keys):
    requests, count, _ = keys.shape
    return pl.pallas_call(
        turn_kernel,
        in_specs=[pl.BlockSpec(memory_space=pltpu.HBM)],
        out_specs=pl.BlockSpec(memory_space=pltpu.VMEM),
        out_shape=jax.ShapeDtypeStruct((requests, HD, count), BF16),
        scratch_shapes=[
            pltpu.VMEM((requests, count, HD), BF16),
            pltpu.SemaphoreType.DMA((requests,)),
        ],
        compiler_params=pltpu.CompilerParams(vmem_limit_bytes=8 << 20),
        name="turn",
    )(pltpu.with_memory_space_constraint(keys, pltpu.HBM))


def cache_kernel(
    len_ref, q_ref, kt_hbm, v_hbm, kv_ref, out_ref, first_scr, second_scr, k_buf, v_buf, sems
):
    requests, _, keys = k_buf.shape

    def fetch_keys(r):
        return pltpu.make_async_copy(kt_hbm.at[r], k_buf.at[r], sems.at[0, r])

    def fetch_values(r):
        return pltpu.make_async_copy(v_hbm.at[r], v_buf.at[r], sems.at[1, r])

    for r in range(requests):
        fetch_keys(r).start()
        fetch_values(r).start()
    start = lax.axis_index(SEQ) * (keys // 2)
    rows = 16 * GROUP
    step = 256
    kv_own = kv_ref[...].astype(F32)
    odd = lax.broadcasted_iota(jnp.int32, (rows, HD), 1) % 2 == 1
    lane = lax.broadcasted_iota(jnp.int32, (8, HD), 1)
    column = lax.broadcasted_iota(jnp.int32, (1, step), 1)
    first_head = (column % 2 == 0).astype(F32).astype(BF16)
    second_head = (column % 2 == 1).astype(F32).astype(BF16)

    def score(r, scr):
        block = q_ref[r * GROUP : (r + 1) * GROUP]
        queries = jnp.concatenate(
            [block[:, 0:16, :].reshape(rows, HD), block[:, 16:32, :].reshape(rows, HD)], axis=1
        )
        limit = 2 * (len_ref[r] - start)
        folded = None
        for c in range(0, keys, step):
            turned = k_buf[r, :, c : c + step]
            both = jnp.concatenate([turned * first_head, turned * second_head], axis=0)
            part = contract(queries, both, ((1,), (0,))) * SCALE2
            part = part + jnp.where(column + c < limit, 0.0, MASKED)
            scr[:, c : c + step] = part
            for d in range(0, step, HD):
                piece = part[:, d : d + HD]
                folded = piece if folded is None else jnp.maximum(folded, piece)
        return folded

    def blend(r, scr, folded):
        s0 = shift_of(jnp.max(jnp.where(odd, MASKED, folded), axis=1, keepdims=True))
        s1 = shift_of(jnp.max(jnp.where(odd, folded, MASKED), axis=1, keepdims=True))
        shift = jnp.where(odd, s1, s0)
        total = jnp.zeros((rows, HD), F32)
        mixed = jnp.zeros((rows, 2 * HD), F32)
        for c in range(0, keys, step):
            pieces = []
            for d in range(c, c + step, HD):
                w = jnp.exp2(scr[:, d : d + HD] - shift)
                total = total + w
                pieces.append(w.astype(BF16))
            mixed = mixed + contract(
                jnp.concatenate(pieces, axis=1),
                head_halves(v_buf[r, c : c + step, :]),
                ((1,), (0,)),
            )
        l0 = jnp.sum(jnp.where(odd, 0.0, total), axis=1, keepdims=True)
        l1 = jnp.sum(jnp.where(odd, total, 0.0), axis=1, keepdims=True)
        stats = stat_tile(s0, s1, l0, l1)
        for j in range(GROUP):
            low, high, at = 16 * j, 16 * j + 16, r * GROUP + j
            out_ref[at, 0:16, :] = mixed[low:high, 0:HD].astype(BF16)
            out_ref[at, 16:32, :] = mixed[low:high, HD:].astype(BF16)
            pair = jnp.where(lane % 2 == 0, stats[low : low + 8], stats[low + 8 : high])
            out_ref[at, 32:48, :] = jnp.concatenate([pair, kv_own], axis=0).astype(BF16)

    scratch = (first_scr, second_scr)
    fetch_keys(0).wait()
    folded = score(0, scratch[0])
    for r in range(requests):
        if r + 1 < requests:
            fetch_keys(r + 1).wait()
        fetch_values(r).wait()
        ahead = score(r + 1, scratch[(r + 1) % 2]) if r + 1 < requests else None
        blend(r, scratch[r % 2], folded)
        folded = ahead


def cache_attend(lengths, queries, keys, values, kv_own):
    requests, _, count = keys.shape
    vmem = pl.BlockSpec(memory_space=pltpu.VMEM)
    return pl.pallas_call(
        cache_kernel,
        in_specs=[
            pl.BlockSpec(memory_space=pltpu.SMEM),
            vmem,
            pl.BlockSpec(memory_space=pltpu.HBM),
            pl.BlockSpec(memory_space=pltpu.HBM),
            vmem,
        ],
        out_specs=vmem,
        out_shape=jax.ShapeDtypeStruct((requests * GROUP, 48, HD), BF16),
        scratch_shapes=[
            pltpu.VMEM((16 * GROUP, count), F32),
            pltpu.VMEM((16 * GROUP, count), F32),
            pltpu.VMEM((requests, HD, count), BF16),
            pltpu.VMEM((requests, count, HD), BF16),
            pltpu.SemaphoreType.DMA((2, requests)),
        ],
        compiler_params=pltpu.CompilerParams(vmem_limit_bytes=20 << 20),
        name="cache_attend",
    )(
        lengths,
        queries,
        pltpu.with_memory_space_constraint(keys, pltpu.HBM),
        pltpu.with_memory_space_constraint(values, pltpu.HBM),
        kv_own,
    )


def merge_kernel(parts_ref, q_ref, anc_ref, out_ref):
    place = lax.axis_index(SEQ)
    request = place // GROUP
    node = 2 * (place % GROUP)
    first = pl.multiple_of(request * GROUP, GROUP)
    tree = parts_ref[pl.ds(first, GROUP), 32:48, :].astype(F32)[:, 8:16, :].reshape(64, HD)
    tree_values = pltpu.roll(tree, 60, 0)
    tree_keys = tree.astype(BF16)
    row = lax.broadcasted_iota(jnp.int32, (32, 64), 0)
    col = lax.broadcasted_iota(jnp.int32, (32, 64), 1)
    picks = (
        lax.broadcasted_iota(jnp.int32, (16, 64), 0)
        == 2 * (lax.broadcasted_iota(jnp.int32, (16, 64), 1) // 8)
        + lax.broadcasted_iota(jnp.int32, (16, 64), 1) % 2
    )
    ancestry = contract(
        anc_ref[request].astype(F32).astype(BF16), picks.astype(F32).astype(BF16), ((1,), (0,))
    )
    which = lax.broadcasted_iota(jnp.int32, (16, 64), 0)
    mine0 = jnp.sum(jnp.where(which == node, ancestry, 0.0), axis=0, keepdims=True)
    mine1 = jnp.sum(jnp.where(which == node + 1, ancestry, 0.0), axis=0, keepdims=True)
    seen = jnp.where((row // 8) % 2 == 0, mine0, mine1)
    allowed = (seen > 0.5) & ((col // 4) % 2 == 0) & ((col // 2) % 2 == row // 16)
    scores = contract(q_ref[...], tree_keys, ((1,), (1,))) * SCALE2
    scores = jnp.where(allowed, scores, MASKED)
    m_tree = jnp.max(scores, axis=1, keepdims=True)
    w_tree = jnp.where(allowed, jnp.exp2(scores - m_tree), 0.0)
    l_tree = jnp.sum(w_tree, axis=1, keepdims=True)
    o_tree = contract(w_tree.astype(BF16), tree_values.astype(BF16), ((1,), (0,)))

    stats = parts_ref[:, 32:48, :].astype(F32)[:, 0:8, :]
    highest = jnp.max(stats, axis=0)
    factor = jnp.exp2(jnp.minimum(stats - highest[None], 0.0))
    sums = pltpu.roll(stats.reshape(-1, HD), 64, 1).reshape(stats.shape)
    total = jnp.sum(sums * factor, axis=0)
    for h in range(2):
        both = parts_ref[:, 16 * h : 16 * h + 16, :].astype(F32)
        for i in range(2):
            lane = h * 32 + i
            at = 16 * h + 8 * i
            blend = jnp.sum(both[:, 8 * i : 8 * i + 8, :] * factor[:, :, lane : lane + 1], axis=0)
            m_far = highest[:, lane : lane + 1]
            m_near = m_tree[at : at + 8]
            top = jnp.maximum(m_far, m_near)
            f_far = jnp.exp2(m_far - top)
            f_near = jnp.exp2(m_near - top)
            denominator = total[:, lane : lane + 1] * f_far + l_tree[at : at + 8] * f_near
            heads = (blend * f_far + o_tree[at : at + 8] * f_near) / denominator
            for g in range(8):
                out_ref[i : i + 1, (8 * h + g) * HD : (8 * h + g + 1) * HD] = heads[g : g + 1]


def merge_lower(parts, own_q, ancestors):
    return pl.pallas_call(
        merge_kernel,
        in_specs=[pl.BlockSpec(memory_space=pltpu.VMEM)] * 3,
        out_specs=pl.BlockSpec(memory_space=pltpu.VMEM),
        out_shape=jax.ShapeDtypeStruct((2, 16 * HD), F32),
        compiler_params=pltpu.CompilerParams(vmem_limit_bytes=8 << 20),
        name="merge_lower",
    )(parts, own_q, ancestors)


def project_kernel(hidden_ref, terms_ref, gain_ref, wq_ref, wk_ref, wv_ref, res_ref, out_ref):
    residual = hidden_ref[...].astype(F32) + terms_ref[...]
    res_ref[...] = residual
    square = jnp.sum(residual * residual, axis=1, keepdims=True)
    coarse = square.astype(BF16).astype(F32)
    lane = lax.broadcasted_iota(jnp.int32, residual.shape, 1)
    squares = jnp.where(lane < 64, coarse, square - coarse).astype(BF16)
    scaled = (residual * gain_ref[...]).astype(BF16)
    q = contract(scaled, wq_ref[...], ((1,), (0,))).astype(BF16)
    k = contract(scaled, wk_ref[...], ((1,), (0,))).astype(BF16)
    v = contract(scaled, wv_ref[...], ((1,), (0,))).astype(BF16)
    tails = [k[:, :HD], squares, k[:, HD:], squares, v[:, :HD], squares, v[:, HD:], squares]
    for r in range(8):
        rows = slice(16 * r, 16 * r + 16)
        for j in range(GROUP):
            at = r * GROUP + j
            out_ref[at, 0:16, :] = q[rows, 2 * j * HD : (2 * j + 1) * HD]
            out_ref[at, 16:32, :] = q[rows, (2 * j + 1) * HD : (2 * j + 2) * HD]
            out_ref[at, 32:48, :] = tails[j][rows]


def project(hidden, terms, gain, wq, wk, wv):
    rows = hidden.shape[0]
    return pl.pallas_call(
        project_kernel,
        out_shape=(
            jax.ShapeDtypeStruct((rows, HD), F32),
            jax.ShapeDtypeStruct((rows // 2, 48, HD), BF16),
        ),
        compiler_params=pltpu.CompilerParams(vmem_limit_bytes=8 << 20),
        name="project",
    )(hidden, terms, gain, wq, wk, wv)


def retained_kernel(
    width, len_ref, g_ref, k_ref, v_ref, pos_ref, anc_ref, out_ref, blend_scr, stat_scr
):
    place = lax.axis_index(SEQ)
    request = place // GROUP
    leader = place % GROUP == 0
    length = len_ref[request]
    kept = (pos_ref[...] < length).astype(F32)
    row = lax.broadcasted_iota(jnp.int32, (HD, 2 * HD), 0)
    col = lax.broadcasted_iota(jnp.int32, (HD, 2 * HD), 1)
    doubled = (row == col // 2).astype(F32).astype(BF16)
    pick_odd = lax.broadcasted_iota(jnp.int32, (1, 2 * HD), 1) % 2 == 1
    kept = jnp.concatenate([kept, jnp.zeros((6, kept.shape[1]), F32)], axis=0).astype(BF16)
    limits = []
    for c in range(0, kept.shape[1], HD):
        wide = contract(kept[:, c : c + HD], doubled, ((1,), (0,)))
        limits.append(jnp.where(pick_odd, wide[1:2], wide[0:1]))
    usable = jnp.concatenate(limits, axis=1)
    tile = g_ref[1, 32:48, :].astype(F32)
    square = tile[:, 0:1] + tile[:, 64:65]
    inverse = lax.rsqrt(square / width + EPS)

    def up(j, at):
        return (g_ref[j, at : at + 16, :].astype(F32) * inverse).astype(BF16)

    def stacked(h):
        return jnp.concatenate(
            [up((8 * h + g) // 2, 16 * ((8 * h + g) % 2)) for g in range(8)], axis=0
        )

    zero = jnp.zeros((16, HD), BF16)
    queries = jnp.concatenate([stacked(0), stacked(1)], axis=1)

    def near(first, second):
        return jnp.concatenate(
            [jnp.concatenate([first, zero], axis=1), jnp.concatenate([zero, second], axis=1)],
            axis=0,
        )

    near_keys = near(up(0, 32), up(2, 32))
    near_values = near(up(4, 32), up(6, 32))
    far = contract(queries, head_halves(k_ref[...]), ((1,), (1,))) * SCALE2
    far = far + jnp.where(usable > 0.5, 0.0, MASKED)
    row_pick = (
        lax.broadcasted_iota(jnp.int32, (128, 16), 0) % 16
        == lax.broadcasted_iota(jnp.int32, (128, 16), 1)
    )
    col_pick = (
        lax.broadcasted_iota(jnp.int32, (16, 32), 1) % 16
        == lax.broadcasted_iota(jnp.int32, (16, 32), 0)
    )
    ancestry = anc_ref[request].astype(F32).astype(BF16)
    seen = contract(ancestry, col_pick.astype(F32).astype(BF16), ((1,), (0,)))
    seen = contract(row_pick.astype(F32).astype(BF16), seen.astype(BF16), ((1,), (0,)))
    close = contract(queries, near_keys, ((1,), (1,))) * SCALE2
    close = jnp.where((seen > 0.5) & leader, close, MASKED)
    second = lax.broadcasted_iota(jnp.int32, close.shape, 1) >= 16
    n0 = jnp.max(jnp.where(second, MASKED, close), axis=1, keepdims=True)
    n1 = jnp.max(jnp.where(second, close, MASKED), axis=1, keepdims=True)
    m0, m1, odd = pair_max(far)
    s0, s1 = shift_of(jnp.maximum(m0, n0)), shift_of(jnp.maximum(m1, n1))
    weights, l0, l1 = pair_weights(far, s0, s1, odd)
    close_w = jnp.exp2(close - jnp.where(second, s1, s0))
    l0 = l0 + jnp.sum(jnp.where(second, 0.0, close_w), axis=1, keepdims=True)
    l1 = l1 + jnp.sum(jnp.where(second, close_w, 0.0), axis=1, keepdims=True)
    blend = contract(weights, head_halves(v_ref[...]), ((1,), (0,)))
    blend = blend + contract(close_w.astype(BF16), near_values, ((1,), (0,)))
    lane = lax.broadcasted_iota(jnp.int32, (128, HD), 1)
    stats = [jnp.where(lane < 64, s0, l0), jnp.where(lane < 64, s1, l1)]
    for h in range(2):
        for g in range(8):
            for half in range(2):
                at = 16 * g + 8 * half
                to = pl.ds(8 * half * 16 + 8 * h + g, 8, stride=16)
                blend_scr[to, :] = blend[at : at + 8, h * HD : (h + 1) * HD]
                stat_scr[to, :] = stats[h][at : at + 8]
    lane = lax.broadcasted_iota(jnp.int32, (16, HD), 1)
    for j in range(GROUP):
        out_ref[j, 0:32, :] = blend_scr[32 * j : 32 * j + 32, :].astype(BF16)
        out_ref[j, 32:48, :] = jnp.where(
            lane % 2 == 0, stat_scr[32 * j : 32 * j + 16, :], stat_scr[32 * j + 16 : 32 * j + 32, :]
        ).astype(BF16)


def retained_attend(width, lengths, gathered, keys, values, positions, ancestors):
    vmem = pl.BlockSpec(memory_space=pltpu.VMEM)
    return pl.pallas_call(
        functools.partial(retained_kernel, width),
        in_specs=[pl.BlockSpec(memory_space=pltpu.SMEM), vmem, vmem, vmem, vmem, vmem],
        out_specs=vmem,
        out_shape=jax.ShapeDtypeStruct((GROUP, 48, HD), BF16),
        scratch_shapes=[pltpu.VMEM((256, HD), F32), pltpu.VMEM((256, HD), F32)],
        compiler_params=pltpu.CompilerParams(vmem_limit_bytes=8 << 20),
        name="retained_attend",
    )(lengths, gathered, keys, values, positions, ancestors)


def finish_kernel(parts_ref, out_ref):
    stats = parts_ref[:, 32:48, :].astype(F32)
    highest = jnp.max(stats, axis=0)
    factor = jnp.exp2(jnp.minimum(stats - highest[None], 0.0))
    sums = pltpu.roll(stats.reshape(-1, HD), 64, 1).reshape(stats.shape)
    total = jnp.sum(sums * factor, axis=0)
    for i in range(2):
        rows = parts_ref[:, 16 * i : 16 * i + 16, :].astype(F32)
        blend = jnp.sum(rows * factor[:, :, i : i + 1], axis=0)
        heads = blend / total[:, i : i + 1]
        for c in range(16):
            out_ref[i : i + 1, c * HD : (c + 1) * HD] = heads[c : c + 1]


def finish_upper(parts):
    return pl.pallas_call(
        finish_kernel,
        out_shape=jax.ShapeDtypeStruct((2, 16 * HD), F32),
        name="finish_upper",
    )(parts)


def swapped(array, axis):
    return lax.ppermute(array, axis, [(0, 1), (1, 0)])


def shards(
    tree_hidden,
    query_low,
    key_tree_low,
    value_tree_low,
    cache_keys,
    cache_values,
    cache_lengths,
    ancestors,
    out_weight,
    norm_gain,
    w_query_up,
    w_key_up,
    w_value_up,
    retained_keys,
    retained_values,
    retained_index,
):
    seq_count = lax.axis_size(SEQ)
    requests, cache_part, kv_heads, _ = cache_keys.shape
    kept = retained_keys.shape[1]
    width = tree_hidden.shape[1] * seq_count
    own_q = query_low.reshape(2, 2, 8, HD).transpose(1, 0, 2, 3).reshape(32, HD)
    kv_own = jnp.concatenate(
        [
            key_tree_low.reshape(2, 2, HD).transpose(1, 0, 2).reshape(4, HD),
            value_tree_low.reshape(2, 2, HD).transpose(1, 0, 2).reshape(4, HD),
        ],
        axis=0,
    )
    queries = spread(own_q, SEQ)
    turned_keys = turn(cache_keys.reshape(requests, cache_part * kv_heads, HD))
    parts = cache_attend(
        cache_lengths,
        queries,
        turned_keys,
        cache_values.reshape(requests, cache_part * kv_heads, HD),
        kv_own,
    )
    own_heads = merge_lower(exchanged(parts, SEQ), own_q, ancestors)
    lower_all = spread(own_heads.astype(BF16), SEQ).reshape(2 * seq_count, -1)
    terms = jnp.dot(lower_all, out_weight, preferred_element_type=F32)
    terms = terms + swapped(terms, "c")
    terms = terms + swapped(terms, "yl")
    residual, projected = project(
        tree_hidden, terms, norm_gain.reshape(1, -1), w_query_up, w_key_up, w_value_up
    )
    summed = jnp.sum(exchanged(projected, SEQ).astype(F32), axis=0).astype(BF16)
    gathered = spread(summed, TEAM)
    upper = retained_attend(
        width,
        cache_lengths,
        gathered,
        retained_keys.reshape(kept * kv_heads, HD),
        retained_values.reshape(kept * kv_heads, HD),
        retained_index[0].T,
        ancestors,
    )
    upper_heads = finish_upper(exchanged(upper, TEAM))
    return (residual, upper_heads)


def solution(mesh):
    fine = Mesh(
        mesh.devices.reshape(4, 2, 4, 2, 2, 2), ("x", "zh", "zl", "yh", "yl", "c")
    )
    seq, tp = SEQ, ("yl", "c")
    return jax.shard_map(
        shards,
        mesh=fine,
        in_specs=(
            P(None, seq),
            P(seq, tp),
            P(seq, tp),
            P(seq, tp),
            P(None, seq, tp, None),
            P(None, seq, tp, None),
            P(),
            P(),
            P(tp, seq),
            P(seq),
            P(seq, tp),
            P(seq, tp),
            P(seq, tp),
            P(seq, None, tp, None),
            P(seq, None, tp, None),
            P(seq, None, tp),
        ),
        out_specs=(P(None, seq), P(seq, tp)),
        check_vma=False,
    )
```

```python
import functools

import jax
import jax.numpy as jnp
from jax import lax
from jax.experimental import pallas as pl
from jax.experimental.pallas import tpu as pltpu
from jax.sharding import Mesh, PartitionSpec as P

HD = 128
GROUP = 8
SCALE = HD ** (-0.5)
SCALE2 = SCALE * 1.4426950408889634
MASKED = -1e30
FLOOR = -1e20
EPS = 1e-05
F32 = jnp.float32
BF16 = jnp.bfloat16

SEQ = ("x", "zh", "zl", "yh")
TEAM = ("zl", "yh")
DEPTH = ("zh", "zl")
FACE = ("x", "yh")
SIDE = ("zh", "zl", "yh")


def contract(a, b, dims):
    return lax.dot_general(a, b, (dims, ((), ())), preferred_element_type=F32)


def exchanged(blocks, axis):
    return lax.all_to_all(blocks, axis, split_axis=0, concat_axis=0, tiled=True)


def spread(array, axis):
    copies = jnp.broadcast_to(array, (lax.axis_size(axis), *array.shape))
    return exchanged(copies, axis)


def head_halves(rows):
    parity = lax.broadcasted_iota(jnp.int32, (16, HD), 0) % 2
    even = (parity == 0).astype(F32).astype(BF16)
    odd = (parity == 1).astype(F32).astype(BF16)
    count = rows.shape[0] // 16
    tiles = rows.reshape(count, 16, HD)
    first = (tiles * even[None]).reshape(rows.shape)
    second = (tiles * odd[None]).reshape(rows.shape)
    return jnp.concatenate([first, second], axis=1)


def pair_max(scores):
    width = scores.shape[1]
    folded = scores[:, 0:HD]
    for c in range(HD, width, HD):
        folded = jnp.maximum(folded, scores[:, c : c + HD])
    odd = lax.broadcasted_iota(jnp.int32, folded.shape, 1) % 2 == 1
    m0 = jnp.max(jnp.where(odd, MASKED, folded), axis=1, keepdims=True)
    m1 = jnp.max(jnp.where(odd, folded, MASKED), axis=1, keepdims=True)
    return m0, m1, odd


def shift_of(maximum):
    return jnp.maximum(maximum, FLOOR).astype(BF16).astype(F32)


def pair_weights(scores, s0, s1, odd):
    width = scores.shape[1]
    shift = jnp.where(odd, s1, s0)
    pieces = []
    total = jnp.zeros((scores.shape[0], HD), F32)
    for c in range(0, width, HD):
        w = jnp.exp2(scores[:, c : c + HD] - shift)
        total = total + w
        pieces.append(w.astype(BF16))
    l0 = jnp.sum(jnp.where(odd, 0.0, total), axis=1, keepdims=True)
    l1 = jnp.sum(jnp.where(odd, total, 0.0), axis=1, keepdims=True)
    return jnp.concatenate(pieces, axis=1), l0, l1


def stat_tile(s0, s1, l0, l1):
    lane = lax.broadcasted_iota(jnp.int32, (s0.shape[0], HD), 1)
    return jnp.where(
        lane < 64, jnp.where(lane < 32, s0, s1), jnp.where(lane < 96, l0, l1)
    )


def turn_kernel(k_hbm, kt_ref, k_buf, sems):
    requests, keys, _ = k_buf.shape
    step = 256

    def copy(r):
        return pltpu.make_async_copy(k_hbm.at[r], k_buf.at[r], sems.at[r])

    for r in range(requests):
        copy(r).start()
    for r in range(requests):
        copy(r).wait()
        for c in range(0, keys, step):
            kt_ref[r, :, c : c + step] = k_buf[r, c : c + step, :].T


def turn(keys):
    requests, count, _ = keys.shape
    return pl.pallas_call(
        turn_kernel,
        in_specs=[pl.BlockSpec(memory_space=pltpu.HBM)],
        out_specs=pl.BlockSpec(memory_space=pltpu.VMEM),
        out_shape=jax.ShapeDtypeStruct((requests, HD, count), BF16),
        scratch_shapes=[
            pltpu.VMEM((requests, count, HD), BF16),
            pltpu.SemaphoreType.DMA((requests,)),
        ],
        compiler_params=pltpu.CompilerParams(vmem_limit_bytes=8 << 20),
        name="turn",
    )(pltpu.with_memory_space_constraint(keys, pltpu.HBM))


def cache_kernel(
    len_ref, q_ref, kt_hbm, v_hbm, kv_ref, out_ref, first_scr, second_scr, k_buf, v_buf, sems
):
    requests, _, keys = k_buf.shape

    def fetch_keys(r):
        return pltpu.make_async_copy(kt_hbm.at[r], k_buf.at[r], sems.at[0, r])

    def fetch_values(r):
        return pltpu.make_async_copy(v_hbm.at[r], v_buf.at[r], sems.at[1, r])

    for r in range(requests):
        fetch_keys(r).start()
        fetch_values(r).start()
    start = lax.axis_index(SEQ) * (keys // 2)
    rows = 16 * GROUP
    step = 256
    kv_own = kv_ref[...].astype(F32)
    odd = lax.broadcasted_iota(jnp.int32, (rows, HD), 1) % 2 == 1
    lane = lax.broadcasted_iota(jnp.int32, (rows, HD), 1)
    kept = {}
    column = lax.broadcasted_iota(jnp.int32, (1, step), 1)
    first_head = (column % 2 == 0).astype(F32).astype(BF16)
    second_head = (column % 2 == 1).astype(F32).astype(BF16)

    def score(r, scr):
        def half(h):
            return jnp.concatenate(
                [
                    q_ref[2 * (r // 2) + j % 2, 4 * (r % 2) + j // 2, 16 * h : 16 * h + 16, :]
                    for j in range(GROUP)
                ],
                axis=0,
            )

        queries = jnp.concatenate([half(0), half(1)], axis=1)
        limit = 2 * (len_ref[r] - start)
        folded = None
        for c in range(0, keys, step):
            turned = k_buf[r, :, c : c + step]
            both = jnp.concatenate([turned * first_head, turned * second_head], axis=0)
            part = contract(queries, both, ((1,), (0,))) * SCALE2
            part = part + jnp.where(column + c < limit, 0.0, MASKED)
            scr[:, c : c + step] = part
            for d in range(0, step, HD):
                piece = part[:, d : d + HD]
                folded = piece if folded is None else jnp.maximum(folded, piece)
        return folded

    def blend(r, scr, folded):
        s0 = shift_of(jnp.max(jnp.where(odd, MASKED, folded), axis=1, keepdims=True))
        s1 = shift_of(jnp.max(jnp.where(odd, folded, MASKED), axis=1, keepdims=True))
        shift = jnp.where(odd, s1, s0)
        total = jnp.zeros((rows, HD), F32)
        mixed = jnp.zeros((rows, 2 * HD), F32)
        for c in range(0, keys, step):
            pieces = []
            for d in range(c, c + step, HD):
                w = jnp.exp2(scr[:, d : d + HD] - shift)
                total = total + w
                pieces.append(w.astype(BF16))
            mixed = mixed + contract(
                jnp.concatenate(pieces, axis=1),
                head_halves(v_buf[r, c : c + step, :]),
                ((1,), (0,)),
            )
        l0 = jnp.sum(jnp.where(odd, 0.0, total), axis=1, keepdims=True)
        l1 = jnp.sum(jnp.where(odd, total, 0.0), axis=1, keepdims=True)
        columns = jnp.where(
            lane < 2, jnp.where(lane == 0, s0, l0), jnp.where(lane == 2, s1, l1)
        )
        kept[r] = columns.T
        for h in range(2):
            at = 2 * (r // 2) + h
            low = 16 * GROUP * (r % 2)
            out_ref[at, low : low + rows, :] = mixed[:, h * HD : (h + 1) * HD].astype(BF16)
            if r % 2 == 1:
                tile = jnp.concatenate(
                    [
                        kept[r - 1][2 * h : 2 * h + 2],
                        kept[r][2 * h : 2 * h + 2],
                        kv_own[2 * h : 2 * h + 2],
                        kv_own[4 + 2 * h : 6 + 2 * h],
                        jnp.zeros((8, HD), F32),
                    ],
                    axis=0,
                )
                out_ref[at, 2 * rows : 2 * rows + 16, :] = tile.astype(BF16)

    scratch = (first_scr, second_scr)
    fetch_keys(0).wait()
    folded = score(0, scratch[0])
    for r in range(requests):
        if r + 1 < requests:
            fetch_keys(r + 1).wait()
        fetch_values(r).wait()
        ahead = score(r + 1, scratch[(r + 1) % 2]) if r + 1 < requests else None
        blend(r, scratch[r % 2], folded)
        folded = ahead


def cache_attend(lengths, queries, keys, values, kv_own):
    requests, _, count = keys.shape
    vmem = pl.BlockSpec(memory_space=pltpu.VMEM)
    return pl.pallas_call(
        cache_kernel,
        in_specs=[
            pl.BlockSpec(memory_space=pltpu.SMEM),
            vmem,
            pl.BlockSpec(memory_space=pltpu.HBM),
            pl.BlockSpec(memory_space=pltpu.HBM),
            vmem,
        ],
        out_specs=vmem,
        out_shape=jax.ShapeDtypeStruct((GROUP, 32 * GROUP + 16, HD), BF16),
        scratch_shapes=[
            pltpu.VMEM((16 * GROUP, count), F32),
            pltpu.VMEM((16 * GROUP, count), F32),
            pltpu.VMEM((requests, HD, count), BF16),
            pltpu.VMEM((requests, count, HD), BF16),
            pltpu.SemaphoreType.DMA((2, requests)),
        ],
        compiler_params=pltpu.CompilerParams(vmem_limit_bytes=20 << 20),
        name="cache_attend",
    )(
        lengths,
        queries,
        pltpu.with_memory_space_constraint(keys, pltpu.HBM),
        pltpu.with_memory_space_constraint(values, pltpu.HBM),
        kv_own,
    )


def folded_parts(parts_ref):
    stats = parts_ref[:, 256:272, :].astype(F32)
    highest = jnp.max(stats, axis=0)
    factor = jnp.exp2(jnp.minimum(stats - highest[None], 0.0))
    columns = factor.reshape(HD, HD).T
    blends, sums = [], []
    for r in range(2):
        mixed = None
        total = None
        for source in range(GROUP):
            at = 16 * source + 2 * r
            part = parts_ref[source, HD * r : HD * r + HD, :].astype(F32) * columns[:, at : at + 1]
            weight = stats[source, 2 * r + 1 : 2 * r + 2] * factor[source, 2 * r : 2 * r + 1]
            mixed = part if mixed is None else mixed + part
            total = weight if total is None else total + weight
        blends.append(mixed)
        sums.append(total)
    return stats, highest, blends, sums


def fold_kernel(parts_ref, out_ref):
    _, highest, blends, sums = folded_parts(parts_ref)
    out_ref[0:HD, :] = blends[0].astype(BF16)
    out_ref[HD : 2 * HD, :] = blends[1].astype(BF16)
    first = 2 * lax.axis_index("x")
    tree0 = parts_ref[first, 256:272, :].astype(F32)[4:8]
    tree1 = parts_ref[first + 1, 256:272, :].astype(F32)[4:8]
    tile = jnp.concatenate(
        [
            highest[0:1],
            sums[0],
            highest[2:3],
            sums[1],
            tree0,
            tree1,
            jnp.zeros((4, HD), F32),
        ],
        axis=0,
    )
    out_ref[2 * HD : 2 * HD + 16, :] = tile.astype(BF16)


def fold_parts(parts):
    return pl.pallas_call(
        fold_kernel,
        in_specs=[pl.BlockSpec(memory_space=pltpu.VMEM)],
        out_specs=pl.BlockSpec(memory_space=pltpu.VMEM),
        out_shape=jax.ShapeDtypeStruct(parts.shape[1:], BF16),
        compiler_params=pltpu.CompilerParams(vmem_limit_bytes=8 << 20),
        name="fold_parts",
    )(parts)


def merge_kernel(parts_ref, q_ref, anc_ref, out_ref, scr):
    x = lax.axis_index("x")
    head = lax.axis_index("yh")
    stats, highest, blends, sums = folded_parts(parts_ref)
    padding = jnp.zeros((HD - 4, HD), F32)
    turned = jnp.concatenate([highest[0:1], sums[0], highest[2:3], sums[1], padding], axis=0).T
    entry = lax.broadcasted_iota(jnp.int32, (16, 64), 1)
    inner = entry % 16 - 4
    is_key = (inner >= 0) & (inner < 8) & (inner % 4 < 2)
    node_of = (entry // 16) * 4 + (inner // 4) * 2 + inner % 4
    pick = (is_key & (node_of == lax.broadcasted_iota(jnp.int32, (16, 64), 0))).astype(F32)
    place = (
        lax.broadcasted_iota(jnp.int32, (HD, 16), 0) // 8
        == lax.broadcasted_iota(jnp.int32, (HD, 16), 1)
    ).astype(F32)
    for r in range(2):
        tree = stats[4 * r : 4 * r + 4].reshape(64, HD)
        values = pltpu.roll(tree, 62, 0).astype(BF16)
        queries = jnp.concatenate(
            [
                jnp.where(
                    head == 0,
                    q_ref[2 * x + j % 2, 4 * r + j // 2, 0:16, :].astype(F32),
                    q_ref[2 * x + j % 2, 4 * r + j // 2, 16:32, :].astype(F32),
                )
                for j in range(GROUP)
            ],
            axis=0,
        ).astype(BF16)
        ancestry = anc_ref[2 * x + r].astype(F32).astype(BF16)
        seen = contract(ancestry, pick.astype(BF16), ((1,), (0,))).astype(BF16)
        seen = contract(place.astype(BF16), seen, ((1,), (0,)))
        scores = contract(queries, tree.astype(BF16), ((1,), (1,))) * SCALE2
        scores = jnp.where(seen > 0.5, scores, MASKED)
        m_near = jnp.max(scores, axis=1, keepdims=True)
        w_near = jnp.where(seen > 0.5, jnp.exp2(scores - m_near), 0.0)
        l_near = jnp.sum(w_near, axis=1, keepdims=True)
        o_near = contract(w_near.astype(BF16), values, ((1,), (0,)))
        m_far = turned[:, 2 * r : 2 * r + 1]
        top = jnp.maximum(m_far, m_near)
        f_far = jnp.exp2(m_far - top)
        f_near = jnp.exp2(m_near - top)
        denominator = turned[:, 2 * r + 1 : 2 * r + 2] * f_far + l_near * f_near
        scr[HD * r : HD * r + HD, :] = (blends[r] * f_far + o_near * f_near) / denominator
    for g in range(8):
        out_ref[:, g * HD : (g + 1) * HD] = scr[pl.ds(g, 32, stride=8), :].astype(BF16)


def merge_lower(parts, queries, ancestors):
    return pl.pallas_call(
        merge_kernel,
        in_specs=[pl.BlockSpec(memory_space=pltpu.VMEM)] * 3,
        out_specs=pl.BlockSpec(memory_space=pltpu.VMEM),
        out_shape=jax.ShapeDtypeStruct((32, 8 * HD), BF16),
        scratch_shapes=[pltpu.VMEM((2 * HD, HD), F32)],
        compiler_params=pltpu.CompilerParams(vmem_limit_bytes=8 << 20),
        name="merge_lower",
    )(parts, queries, ancestors)


def output_kernel(heads_ref, weight_ref, out_ref):
    half = weight_ref.shape[0] // 2
    total = None
    for h in range(2):
        rows = jnp.concatenate([heads_ref[2 * x + h] for x in range(4)], axis=0)
        term = contract(rows, weight_ref[h * half : (h + 1) * half, :], ((1,), (0,)))
        total = term if total is None else total + term
    out_ref[...] = total


def output_terms(heads, weight):
    return pl.pallas_call(
        output_kernel,
        in_specs=[pl.BlockSpec(memory_space=pltpu.VMEM)] * 2,
        out_specs=pl.BlockSpec(memory_space=pltpu.VMEM),
        out_shape=jax.ShapeDtypeStruct((4 * heads.shape[1], weight.shape[1]), F32),
        compiler_params=pltpu.CompilerParams(vmem_limit_bytes=8 << 20),
        name="output_terms",
    )(heads, weight)


def project_kernel(hidden_ref, terms_ref, gain_ref, wq_ref, wk_ref, wv_ref, res_ref, out_ref):
    residual = hidden_ref[...].astype(F32) + terms_ref[...]
    res_ref[...] = residual
    square = jnp.sum(residual * residual, axis=1, keepdims=True)
    coarse = square.astype(BF16).astype(F32)
    lane = lax.broadcasted_iota(jnp.int32, residual.shape, 1)
    squares = jnp.where(lane < 64, coarse, square - coarse).astype(BF16)
    scaled = (residual * gain_ref[...]).astype(BF16)
    q = contract(scaled, wq_ref[...], ((1,), (0,))).astype(BF16)
    k = contract(scaled, wk_ref[...], ((1,), (0,))).astype(BF16)
    v = contract(scaled, wv_ref[...], ((1,), (0,))).astype(BF16)
    for h in range(2):
        blocks = [q[:, (8 * h + g) * HD : (8 * h + g + 1) * HD] for g in range(8)]
        blocks += [k[:, h * HD : (h + 1) * HD], v[:, h * HD : (h + 1) * HD], squares]
        for r in range(8):
            for b, block in enumerate(blocks):
                at = (r % 2) * 176 + 16 * b
                out_ref[2 * (r // 2) + h, at : at + 16, :] = block[16 * r : 16 * r + 16]


def project(hidden, terms, gain, wq, wk, wv):
    rows = hidden.shape[0]
    return pl.pallas_call(
        project_kernel,
        out_shape=(
            jax.ShapeDtypeStruct((rows, HD), F32),
            jax.ShapeDtypeStruct((GROUP, 352, HD), BF16),
        ),
        compiler_params=pltpu.CompilerParams(vmem_limit_bytes=8 << 20),
        name="project",
    )(hidden, terms, gain, wq, wk, wv)


def retained_kernel(
    width, len_ref, g_ref, k_ref, v_ref, pos_ref, anc_ref, out_ref, blend_scr, stat_scr
):
    place = lax.axis_index(SEQ)
    request = place // GROUP
    leader = place % GROUP == 0
    length = len_ref[request]
    kept = (pos_ref[...] < length).astype(F32)
    row = lax.broadcasted_iota(jnp.int32, (HD, 2 * HD), 0)
    col = lax.broadcasted_iota(jnp.int32, (HD, 2 * HD), 1)
    doubled = (row == col // 2).astype(F32).astype(BF16)
    pick_odd = lax.broadcasted_iota(jnp.int32, (1, 2 * HD), 1) % 2 == 1
    kept = jnp.concatenate([kept, jnp.zeros((6, kept.shape[1]), F32)], axis=0).astype(BF16)
    limits = []
    for c in range(0, kept.shape[1], HD):
        wide = contract(kept[:, c : c + HD], doubled, ((1,), (0,)))
        limits.append(jnp.where(pick_odd, wide[1:2], wide[0:1]))
    usable = jnp.concatenate(limits, axis=1)
    raw = []
    for h in range(2):
        total = g_ref[h].astype(F32)
        for z in range(1, GROUP):
            total = total + g_ref[2 * z + h].astype(F32)
        raw.append(total)
    square = raw[0][160:176, 0:1] + raw[0][160:176, 64:65]
    inverse = lax.rsqrt(square / width + EPS)

    def up(h, b):
        return (raw[h][16 * b : 16 * b + 16] * inverse).astype(BF16)

    def stacked(h):
        return jnp.concatenate([up(h, g) for g in range(8)], axis=0)

    zero = jnp.zeros((16, HD), BF16)
    queries = jnp.concatenate([stacked(0), stacked(1)], axis=1)

    def near(first, second):
        return jnp.concatenate(
            [jnp.concatenate([first, zero], axis=1), jnp.concatenate([zero, second], axis=1)],
            axis=0,
        )

    near_keys = near(up(0, 8), up(1, 8))
    near_values = near(up(0, 9), up(1, 9))
    far = contract(queries, head_halves(k_ref[...]), ((1,), (1,))) * SCALE2
    far = far + jnp.where(usable > 0.5, 0.0, MASKED)
    row_pick = (
        lax.broadcasted_iota(jnp.int32, (128, 16), 0) % 16
        == lax.broadcasted_iota(jnp.int32, (128, 16), 1)
    )
    col_pick = (
        lax.broadcasted_iota(jnp.int32, (16, 32), 1) % 16
        == lax.broadcasted_iota(jnp.int32, (16, 32), 0)
    )
    ancestry = anc_ref[request].astype(F32).astype(BF16)
    seen = contract(ancestry, col_pick.astype(F32).astype(BF16), ((1,), (0,)))
    seen = contract(row_pick.astype(F32).astype(BF16), seen.astype(BF16), ((1,), (0,)))
    close = contract(queries, near_keys, ((1,), (1,))) * SCALE2
    close = jnp.where((seen > 0.5) & leader, close, MASKED)
    second = lax.broadcasted_iota(jnp.int32, close.shape, 1) >= 16
    n0 = jnp.max(jnp.where(second, MASKED, close), axis=1, keepdims=True)
    n1 = jnp.max(jnp.where(second, close, MASKED), axis=1, keepdims=True)
    m0, m1, odd = pair_max(far)
    s0, s1 = shift_of(jnp.maximum(m0, n0)), shift_of(jnp.maximum(m1, n1))
    weights, l0, l1 = pair_weights(far, s0, s1, odd)
    close_w = jnp.exp2(close - jnp.where(second, s1, s0))
    l0 = l0 + jnp.sum(jnp.where(second, 0.0, close_w), axis=1, keepdims=True)
    l1 = l1 + jnp.sum(jnp.where(second, close_w, 0.0), axis=1, keepdims=True)
    blend = contract(weights, head_halves(v_ref[...]), ((1,), (0,)))
    blend = blend + contract(close_w.astype(BF16), near_values, ((1,), (0,)))
    lane = lax.broadcasted_iota(jnp.int32, (128, HD), 1)
    stats = [jnp.where(lane < 64, s0, l0), jnp.where(lane < 64, s1, l1)]
    for h in range(2):
        for g in range(8):
            for half in range(2):
                at = 16 * g + 8 * half
                to = pl.ds(8 * half * 16 + 8 * h + g, 8, stride=16)
                blend_scr[to, :] = blend[at : at + 8, h * HD : (h + 1) * HD]
                stat_scr[to, :] = stats[h][at : at + 8]
    lane = lax.broadcasted_iota(jnp.int32, (16, HD), 1)
    for j in range(GROUP):
        out_ref[j, 0:32, :] = blend_scr[32 * j : 32 * j + 32, :].astype(BF16)
        out_ref[j, 32:48, :] = jnp.where(
            lane % 2 == 0, stat_scr[32 * j : 32 * j + 16, :], stat_scr[32 * j + 16 : 32 * j + 32, :]
        ).astype(BF16)


def retained_attend(width, lengths, gathered, keys, values, positions, ancestors):
    vmem = pl.BlockSpec(memory_space=pltpu.VMEM)
    return pl.pallas_call(
        functools.partial(retained_kernel, width),
        in_specs=[pl.BlockSpec(memory_space=pltpu.SMEM), vmem, vmem, vmem, vmem, vmem],
        out_specs=vmem,
        out_shape=jax.ShapeDtypeStruct((GROUP, 48, HD), BF16),
        scratch_shapes=[pltpu.VMEM((256, HD), F32), pltpu.VMEM((256, HD), F32)],
        compiler_params=pltpu.CompilerParams(vmem_limit_bytes=8 << 20),
        name="retained_attend",
    )(lengths, gathered, keys, values, positions, ancestors)


def finish_kernel(parts_ref, out_ref):
    stats = parts_ref[:, 32:48, :].astype(F32)
    highest = jnp.max(stats, axis=0)
    factor = jnp.exp2(jnp.minimum(stats - highest[None], 0.0))
    sums = pltpu.roll(stats.reshape(-1, HD), 64, 1).reshape(stats.shape)
    total = jnp.sum(sums * factor, axis=0)
    for i in range(2):
        rows = parts_ref[:, 16 * i : 16 * i + 16, :].astype(F32)
        blend = jnp.sum(rows * factor[:, :, i : i + 1], axis=0)
        heads = blend / total[:, i : i + 1]
        for c in range(16):
            out_ref[i : i + 1, c * HD : (c + 1) * HD] = heads[c : c + 1]


def finish_upper(parts):
    return pl.pallas_call(
        finish_kernel,
        out_shape=jax.ShapeDtypeStruct((2, 16 * HD), F32),
        name="finish_upper",
    )(parts)


def swapped(array, axis):
    return lax.ppermute(array, axis, [(0, 1), (1, 0)])


def shards(
    tree_hidden,
    query_low,
    key_tree_low,
    value_tree_low,
    cache_keys,
    cache_values,
    cache_lengths,
    ancestors,
    out_weight,
    norm_gain,
    w_query_up,
    w_key_up,
    w_value_up,
    retained_keys,
    retained_values,
    retained_index,
):
    seq_count = lax.axis_size(SEQ)
    requests, cache_part, kv_heads, _ = cache_keys.shape
    kept = retained_keys.shape[1]
    width = tree_hidden.shape[1] * seq_count
    own_q = query_low.reshape(2, 2, 8, HD).transpose(1, 0, 2, 3).reshape(32, HD)
    kv_own = jnp.concatenate(
        [
            key_tree_low.reshape(2, 2, HD).transpose(1, 0, 2).reshape(4, HD),
            value_tree_low.reshape(2, 2, HD).transpose(1, 0, 2).reshape(4, HD),
        ],
        axis=0,
    )
    queries = spread(spread(own_q, DEPTH).reshape(-1, HD), FACE).reshape(GROUP, GROUP, 32, HD)
    turned_keys = turn(cache_keys.reshape(requests, cache_part * kv_heads, HD))
    parts = cache_attend(
        cache_lengths,
        queries,
        turned_keys,
        cache_values.reshape(requests, cache_part * kv_heads, HD),
        kv_own,
    )
    folded = spread(fold_parts(exchanged(parts, FACE)), DEPTH)
    heads = merge_lower(folded, queries, ancestors)
    terms = output_terms(spread(heads, FACE), out_weight)
    terms = terms + swapped(terms, "c")
    terms = terms + swapped(terms, "yl")
    residual, projected = project(
        tree_hidden, terms, norm_gain.reshape(1, -1), w_query_up, w_key_up, w_value_up
    )
    summed = jnp.sum(exchanged(projected, FACE).astype(F32), axis=0).astype(BF16)
    shares = jnp.broadcast_to(summed.reshape(2, 1, 176, HD), (2, GROUP, 176, HD))
    gathered = exchanged(shares.reshape(2 * GROUP, 176, HD), SIDE)
    upper = retained_attend(
        width,
        cache_lengths,
        gathered,
        retained_keys.reshape(kept * kv_heads, HD),
        retained_values.reshape(kept * kv_heads, HD),
        retained_index[0].T,
        ancestors,
    )
    upper_heads = finish_upper(exchanged(upper, TEAM))
    return (residual, upper_heads)


def solution(mesh):
    fine = Mesh(
        mesh.devices.reshape(4, 2, 4, 2, 2, 2), ("x", "zh", "zl", "yh", "yl", "c")
    )
    seq, tp = SEQ, ("yl", "c")
    return jax.shard_map(
        shards,
        mesh=fine,
        in_specs=(
            P(None, seq),
            P(seq, tp),
            P(seq, tp),
            P(seq, tp),
            P(None, seq, tp, None),
            P(None, seq, tp, None),
            P(),
            P(),
            P(tp, seq),
            P(seq),
            P(seq, tp),
            P(seq, tp),
            P(seq, tp),
            P(seq, None, tp, None),
            P(seq, None, tp, None),
            P(seq, None, tp),
        ),
        out_specs=(P(None, seq), P(seq, tp)),
        check_vma=False,
    )
```

```python
import functools

import jax
import jax.numpy as jnp
from jax import lax
from jax.experimental import pallas as pl
from jax.experimental.pallas import tpu as pltpu
from jax.sharding import Mesh, PartitionSpec as P

HD = 128
GROUP = 8
SCALE = HD ** (-0.5)
SCALE2 = SCALE * 1.4426950408889634
MASKED = -1e30
FLOOR = -1e20
EPS = 1e-05
F32 = jnp.float32
BF16 = jnp.bfloat16

SEQ = ("x", "zh", "zl", "yh")
TEAM = ("zl", "yh")
DEPTH = ("zh", "zl")
FACE = ("x", "yh")


def contract(a, b, dims):
    return lax.dot_general(a, b, (dims, ((), ())), preferred_element_type=F32)


def exchanged(blocks, axis):
    return lax.all_to_all(blocks, axis, split_axis=0, concat_axis=0, tiled=True)


def spread(array, axis):
    copies = jnp.broadcast_to(array, (lax.axis_size(axis), *array.shape))
    return exchanged(copies, axis)


def head_halves(rows):
    parity = lax.broadcasted_iota(jnp.int32, (16, HD), 0) % 2
    even = (parity == 0).astype(F32).astype(BF16)
    odd = (parity == 1).astype(F32).astype(BF16)
    count = rows.shape[0] // 16
    tiles = rows.reshape(count, 16, HD)
    first = (tiles * even[None]).reshape(rows.shape)
    second = (tiles * odd[None]).reshape(rows.shape)
    return jnp.concatenate([first, second], axis=1)


def shift_of(maximum):
    return jnp.maximum(maximum, FLOOR).astype(BF16).astype(F32)


def turn_kernel(k_hbm, kt_hbm, k_buf, kt_buf, sems):
    requests, keys, _ = k_buf.shape
    step = 256

    def fetch(r):
        return pltpu.make_async_copy(k_hbm.at[r], k_buf.at[r], sems.at[0, r])

    def store(r):
        return pltpu.make_async_copy(kt_buf.at[r], kt_hbm.at[r], sems.at[1, r])

    for r in range(requests):
        fetch(r).start()
    for r in range(requests):
        fetch(r).wait()
        for c in range(0, keys, step):
            kt_buf[r, :, c : c + step] = k_buf[r, c : c + step, :].T
        store(r).start()
    for r in range(requests):
        store(r).wait()


def turn(keys):
    requests, count, _ = keys.shape
    return pl.pallas_call(
        turn_kernel,
        in_specs=[pl.BlockSpec(memory_space=pltpu.HBM)],
        out_specs=pl.BlockSpec(memory_space=pltpu.HBM),
        out_shape=pltpu.HBM((requests, HD, count), BF16),
        scratch_shapes=[
            pltpu.VMEM((requests, count, HD), BF16),
            pltpu.VMEM((requests, HD, count), BF16),
            pltpu.SemaphoreType.DMA((2, requests)),
        ],
        compiler_params=pltpu.CompilerParams(vmem_limit_bytes=12 << 20),
        name="turn",
    )(pltpu.with_memory_space_constraint(keys, pltpu.HBM))


def cache_kernel(
    len_ref, q_ref, kt_hbm, v_hbm, kv_ref, out_ref, first_scr, second_scr, k_buf, v_buf, sems
):
    requests, _, keys = k_buf.shape

    def fetch_keys(r):
        return pltpu.make_async_copy(kt_hbm.at[r], k_buf.at[r], sems.at[0, r])

    def fetch_values(r):
        return pltpu.make_async_copy(v_hbm.at[r], v_buf.at[r], sems.at[1, r])

    for r in range(requests):
        fetch_keys(r).start()
        fetch_values(r).start()
    start = lax.axis_index(SEQ) * (keys // 2)
    rows = 16 * GROUP
    step = 256
    kv_own = kv_ref[...].astype(F32)
    odd = lax.broadcasted_iota(jnp.int32, (rows, HD), 1) % 2 == 1
    lane = lax.broadcasted_iota(jnp.int32, (rows, HD), 1)
    kept = {}
    column = lax.broadcasted_iota(jnp.int32, (1, step), 1)
    first_head = (column % 2 == 0).astype(F32).astype(BF16)
    second_head = (column % 2 == 1).astype(F32).astype(BF16)

    def score(r, scr):
        def half(h):
            return jnp.concatenate(
                [
                    q_ref[2 * (r // 2) + j % 2, 4 * (r % 2) + j // 2, 16 * h : 16 * h + 16, :]
                    for j in range(GROUP)
                ],
                axis=0,
            )

        queries = jnp.concatenate([half(0), half(1)], axis=1)
        limit = 2 * (len_ref[r] - start)
        folded = None
        for c in range(0, keys, step):
            turned = k_buf[r, :, c : c + step]
            both = jnp.concatenate([turned * first_head, turned * second_head], axis=0)
            part = contract(queries, both, ((1,), (0,))) * SCALE2
            part = part + jnp.where(column + c < limit, 0.0, MASKED)
            scr[:, c : c + step] = part
            for d in range(0, step, HD):
                piece = part[:, d : d + HD]
                folded = piece if folded is None else jnp.maximum(folded, piece)
        return folded

    def blend(r, scr, folded):
        s0 = shift_of(jnp.max(jnp.where(odd, MASKED, folded), axis=1, keepdims=True))
        s1 = shift_of(jnp.max(jnp.where(odd, folded, MASKED), axis=1, keepdims=True))
        shift = jnp.where(odd, s1, s0)
        total = jnp.zeros((rows, HD), F32)
        mixed = jnp.zeros((rows, 2 * HD), F32)
        for c in range(0, keys, step):
            pieces = []
            for d in range(c, c + step, HD):
                w = jnp.exp2(scr[:, d : d + HD] - shift)
                total = total + w
                pieces.append(w.astype(BF16))
            mixed = mixed + contract(
                jnp.concatenate(pieces, axis=1),
                head_halves(v_buf[r, c : c + step, :]),
                ((1,), (0,)),
            )
        l0 = jnp.sum(jnp.where(odd, 0.0, total), axis=1, keepdims=True)
        l1 = jnp.sum(jnp.where(odd, total, 0.0), axis=1, keepdims=True)
        columns = jnp.where(
            lane < 2, jnp.where(lane == 0, s0, l0), jnp.where(lane == 2, s1, l1)
        )
        kept[r] = columns.T
        for h in range(2):
            at = 2 * (r // 2) + h
            low = 16 * GROUP * (r % 2)
            out_ref[at, low : low + rows, :] = mixed[:, h * HD : (h + 1) * HD].astype(BF16)
            if r % 2 == 1:
                tile = jnp.concatenate(
                    [
                        kept[r - 1][2 * h : 2 * h + 2],
                        kept[r][2 * h : 2 * h + 2],
                        kv_own[2 * h : 2 * h + 2],
                        kv_own[4 + 2 * h : 6 + 2 * h],
                        jnp.zeros((8, HD), F32),
                    ],
                    axis=0,
                )
                out_ref[at, 2 * rows : 2 * rows + 16, :] = tile.astype(BF16)

    scratch = (first_scr, second_scr)
    fetch_keys(0).wait()
    folded = score(0, scratch[0])
    for r in range(requests):
        if r + 1 < requests:
            fetch_keys(r + 1).wait()
        fetch_values(r).wait()
        ahead = score(r + 1, scratch[(r + 1) % 2]) if r + 1 < requests else None
        blend(r, scratch[r % 2], folded)
        folded = ahead


def cache_attend(lengths, queries, keys, values, kv_own):
    requests, _, count = keys.shape
    vmem = pl.BlockSpec(memory_space=pltpu.VMEM)
    return pl.pallas_call(
        cache_kernel,
        in_specs=[
            pl.BlockSpec(memory_space=pltpu.SMEM),
            vmem,
            pl.BlockSpec(memory_space=pltpu.HBM),
            pl.BlockSpec(memory_space=pltpu.HBM),
            vmem,
        ],
        out_specs=vmem,
        out_shape=jax.ShapeDtypeStruct((GROUP, 32 * GROUP + 16, HD), BF16),
        scratch_shapes=[
            pltpu.VMEM((16 * GROUP, count), F32),
            pltpu.VMEM((16 * GROUP, count), F32),
            pltpu.VMEM((requests, HD, count), BF16),
            pltpu.VMEM((requests, count, HD), BF16),
            pltpu.SemaphoreType.DMA((2, requests)),
        ],
        compiler_params=pltpu.CompilerParams(vmem_limit_bytes=20 << 20),
        name="cache_attend",
    )(
        lengths,
        queries,
        pltpu.with_memory_space_constraint(keys, pltpu.HBM),
        pltpu.with_memory_space_constraint(values, pltpu.HBM),
        kv_own,
    )


def folded_parts(parts_ref):
    stats = parts_ref[:, 256:272, :].astype(F32)
    highest = jnp.max(stats, axis=0)
    factor = jnp.exp2(jnp.minimum(stats - highest[None], 0.0))
    columns = factor.reshape(HD, HD).T
    blends, sums = [], []
    for r in range(2):
        mixed = None
        total = None
        for source in range(GROUP):
            at = 16 * source + 2 * r
            part = parts_ref[source, HD * r : HD * r + HD, :].astype(F32) * columns[:, at : at + 1]
            weight = stats[source, 2 * r + 1 : 2 * r + 2] * factor[source, 2 * r : 2 * r + 1]
            mixed = part if mixed is None else mixed + part
            total = weight if total is None else total + weight
        blends.append(mixed)
        sums.append(total)
    return stats, highest, blends, sums


def fold_kernel(parts_ref, out_ref):
    _, highest, blends, sums = folded_parts(parts_ref)
    out_ref[0:HD, :] = blends[0].astype(BF16)
    out_ref[HD : 2 * HD, :] = blends[1].astype(BF16)
    first = 2 * lax.axis_index("x")
    tree0 = parts_ref[first, 256:272, :].astype(F32)[4:8]
    tree1 = parts_ref[first + 1, 256:272, :].astype(F32)[4:8]
    tile = jnp.concatenate(
        [
            highest[0:1],
            sums[0],
            highest[2:3],
            sums[1],
            tree0,
            tree1,
            jnp.zeros((4, HD), F32),
        ],
        axis=0,
    )
    out_ref[2 * HD : 2 * HD + 16, :] = tile.astype(BF16)


def fold_parts(parts):
    return pl.pallas_call(
        fold_kernel,
        in_specs=[pl.BlockSpec(memory_space=pltpu.VMEM)],
        out_specs=pl.BlockSpec(memory_space=pltpu.VMEM),
        out_shape=jax.ShapeDtypeStruct(parts.shape[1:], BF16),
        compiler_params=pltpu.CompilerParams(vmem_limit_bytes=8 << 20),
        name="fold_parts",
    )(parts)


def merge_kernel(parts_ref, q_ref, anc_ref, out_ref, scr):
    x = lax.axis_index("x")
    head = lax.axis_index("yh")
    stats, highest, blends, sums = folded_parts(parts_ref)
    padding = jnp.zeros((HD - 4, HD), F32)
    turned = jnp.concatenate([highest[0:1], sums[0], highest[2:3], sums[1], padding], axis=0).T
    entry = lax.broadcasted_iota(jnp.int32, (16, 64), 1)
    inner = entry % 16 - 4
    is_key = (inner >= 0) & (inner < 8) & (inner % 4 < 2)
    node_of = (entry // 16) * 4 + (inner // 4) * 2 + inner % 4
    pick = (is_key & (node_of == lax.broadcasted_iota(jnp.int32, (16, 64), 0))).astype(F32)
    place = (
        lax.broadcasted_iota(jnp.int32, (HD, 16), 0) // 8
        == lax.broadcasted_iota(jnp.int32, (HD, 16), 1)
    ).astype(F32)
    for r in range(2):
        tree = stats[4 * r : 4 * r + 4].reshape(64, HD)
        values = pltpu.roll(tree, 62, 0).astype(BF16)
        queries = jnp.concatenate(
            [
                jnp.where(
                    head == 0,
                    q_ref[2 * x + j % 2, 4 * r + j // 2, 0:16, :].astype(F32),
                    q_ref[2 * x + j % 2, 4 * r + j // 2, 16:32, :].astype(F32),
                )
                for j in range(GROUP)
            ],
            axis=0,
        ).astype(BF16)
        ancestry = anc_ref[2 * x + r].astype(F32).astype(BF16)
        seen = contract(ancestry, pick.astype(BF16), ((1,), (0,))).astype(BF16)
        seen = contract(place.astype(BF16), seen, ((1,), (0,)))
        scores = contract(queries, tree.astype(BF16), ((1,), (1,))) * SCALE2
        scores = jnp.where(seen > 0.5, scores, MASKED)
        m_near = jnp.max(scores, axis=1, keepdims=True)
        w_near = jnp.where(seen > 0.5, jnp.exp2(scores - m_near), 0.0)
        l_near = jnp.sum(w_near, axis=1, keepdims=True)
        o_near = contract(w_near.astype(BF16), values, ((1,), (0,)))
        m_far = turned[:, 2 * r : 2 * r + 1]
        top = jnp.maximum(m_far, m_near)
        f_far = jnp.exp2(m_far - top)
        f_near = jnp.exp2(m_near - top)
        denominator = turned[:, 2 * r + 1 : 2 * r + 2] * f_far + l_near * f_near
        scr[HD * r : HD * r + HD, :] = (blends[r] * f_far + o_near * f_near) / denominator
    for g in range(8):
        out_ref[:, g * HD : (g + 1) * HD] = scr[pl.ds(g, 32, stride=8), :].astype(BF16)


def merge_lower(parts, queries, ancestors):
    return pl.pallas_call(
        merge_kernel,
        in_specs=[pl.BlockSpec(memory_space=pltpu.VMEM)] * 3,
        out_specs=pl.BlockSpec(memory_space=pltpu.VMEM),
        out_shape=jax.ShapeDtypeStruct((32, 8 * HD), BF16),
        scratch_shapes=[pltpu.VMEM((2 * HD, HD), F32)],
        compiler_params=pltpu.CompilerParams(vmem_limit_bytes=8 << 20),
        name="merge_lower",
    )(parts, queries, ancestors)


def output_kernel(heads_ref, weight_ref, out_ref):
    half = weight_ref.shape[0] // 2
    total = None
    for h in range(2):
        rows = jnp.concatenate([heads_ref[2 * x + h] for x in range(4)], axis=0)
        term = contract(rows, weight_ref[h * half : (h + 1) * half, :], ((1,), (0,)))
        total = term if total is None else total + term
    out_ref[...] = total


def output_terms(heads, weight):
    return pl.pallas_call(
        output_kernel,
        in_specs=[pl.BlockSpec(memory_space=pltpu.VMEM)] * 2,
        out_specs=pl.BlockSpec(memory_space=pltpu.VMEM),
        out_shape=jax.ShapeDtypeStruct((4 * heads.shape[1], weight.shape[1]), F32),
        compiler_params=pltpu.CompilerParams(vmem_limit_bytes=8 << 20),
        name="output_terms",
    )(heads, weight)


def project_kernel(hidden_ref, terms_ref, gain_ref, wq_ref, wk_ref, wv_ref, res_ref, out_ref):
    residual = hidden_ref[...].astype(F32) + terms_ref[...]
    res_ref[...] = residual
    square = jnp.sum(residual * residual, axis=1, keepdims=True)
    coarse = square.astype(BF16).astype(F32)
    lane = lax.broadcasted_iota(jnp.int32, residual.shape, 1)
    squares = jnp.where(lane < 64, coarse, square - coarse).astype(BF16)
    scaled = (residual * gain_ref[...]).astype(BF16)
    q = contract(scaled, wq_ref[...], ((1,), (0,))).astype(BF16)
    k = contract(scaled, wk_ref[...], ((1,), (0,))).astype(BF16)
    v = contract(scaled, wv_ref[...], ((1,), (0,))).astype(BF16)
    for h in range(2):
        blocks = [q[:, (8 * h + g) * HD : (8 * h + g + 1) * HD] for g in range(8)]
        blocks += [k[:, h * HD : (h + 1) * HD], v[:, h * HD : (h + 1) * HD], squares]
        for r in range(8):
            for b, block in enumerate(blocks):
                at = (r % 2) * 176 + 16 * b
                out_ref[2 * (r // 2) + h, at : at + 16, :] = block[16 * r : 16 * r + 16]


def project(hidden, terms, gain, wq, wk, wv):
    rows = hidden.shape[0]
    return pl.pallas_call(
        project_kernel,
        out_shape=(
            jax.ShapeDtypeStruct((rows, HD), F32),
            jax.ShapeDtypeStruct((GROUP, 352, HD), BF16),
        ),
        compiler_params=pltpu.CompilerParams(vmem_limit_bytes=8 << 20),
        name="project",
    )(hidden, terms, gain, wq, wk, wv)


def split_kernel(len_ref, k_ref, v_ref, pos_ref, mine_ref, give_ref):
    own = lax.axis_index("yh")
    length = len_ref[lax.axis_index(SEQ) // GROUP]
    row = lax.broadcasted_iota(jnp.int32, (2 * HD, 2 * HD), 0)
    col = lax.broadcasted_iota(jnp.int32, (2 * HD, 2 * HD), 1)
    source = 2 * (row % HD) + jnp.where(row < HD, own, 1 - own)
    pick = (col == source).astype(F32).astype(BF16)
    count = k_ref.shape[0] // 2
    for at, ref in ((0, k_ref), (count, v_ref)):
        for c in range(0, count, HD):
            pair = contract(pick, ref[2 * c : 2 * c + 2 * HD, :], ((1,), (0,))).astype(BF16)
            mine_ref[at + c : at + c + HD, :] = pair[0:HD]
            give_ref[at + c : at + c + HD, :] = pair[HD:]
    kept = (pos_ref[...] < length).astype(F32)
    rows0 = [kept[0:1, c : c + HD] for c in range(0, count, HD)]
    rows1 = [kept[1:2, c : c + HD] for c in range(0, count, HD)]
    rest = jnp.zeros((16 - len(rows0), HD), F32)
    limits0 = jnp.concatenate(rows0 + [rest], axis=0)
    limits1 = jnp.concatenate(rows1 + [rest], axis=0)
    mine_ref[2 * count : 2 * count + 16, :] = jnp.where(own == 0, limits0, limits1).astype(BF16)
    give_ref[2 * count : 2 * count + 16, :] = jnp.where(own == 0, limits1, limits0).astype(BF16)


def split_heads(lengths, keys, values, positions):
    count = keys.shape[0]
    vmem = pl.BlockSpec(memory_space=pltpu.VMEM)
    return pl.pallas_call(
        split_kernel,
        in_specs=[pl.BlockSpec(memory_space=pltpu.SMEM), vmem, vmem, vmem],
        out_specs=[vmem, vmem],
        out_shape=[jax.ShapeDtypeStruct((count + 16, HD), BF16)] * 2,
        compiler_params=pltpu.CompilerParams(vmem_limit_bytes=8 << 20),
        name="split_heads",
    )(lengths, keys, values, positions)


def retained_kernel(width, sum_ref, mine_ref, other_ref, anc_ref, out_ref, blend_scr, stat_scr):
    request = lax.axis_index(SEQ) // GROUP
    leader = lax.axis_index("zl") == 0
    raw = sum_ref[...].astype(F32)
    square = raw[160:176, 0:1] + raw[160:176, 64:65]
    inverse = lax.rsqrt(square / width + EPS)

    def up(b):
        return (raw[16 * b : 16 * b + 16] * inverse).astype(BF16)

    queries = jnp.concatenate([up(g) for g in range(8)], axis=0)
    near_keys, near_values = up(8), up(9)
    count = (mine_ref.shape[0] - 16) // 2
    parts = []
    for ref in (mine_ref, other_ref):
        limits = ref[2 * count : 2 * count + 16, :].astype(F32)
        part = contract(queries, ref[0:count, :], ((1,), (1,))) * SCALE2
        for c in range(0, count, HD):
            usable = limits[c // HD : c // HD + 1] > 0.5
            parts.append(jnp.where(usable, part[:, c : c + HD], MASKED))
    row_pick = (
        lax.broadcasted_iota(jnp.int32, (HD, 16), 0) % 16
        == lax.broadcasted_iota(jnp.int32, (HD, 16), 1)
    )
    ancestry = anc_ref[request].astype(F32).astype(BF16)
    seen = contract(row_pick.astype(F32).astype(BF16), ancestry, ((1,), (0,)))
    close = contract(queries, near_keys, ((1,), (1,))) * SCALE2
    close = jnp.where((seen > 0.5) & leader, close, MASKED)
    folded = parts[0]
    for part in parts[1:]:
        folded = jnp.maximum(folded, part)
    top = jnp.maximum(
        jnp.max(folded, axis=1, keepdims=True), jnp.max(close, axis=1, keepdims=True)
    )
    shift = shift_of(top)
    weights = [jnp.exp2(part - shift) for part in parts]
    near_w = jnp.exp2(close - shift)
    total = weights[0]
    for w in weights[1:]:
        total = total + w
    sums = jnp.sum(total, axis=1, keepdims=True) + jnp.sum(near_w, axis=1, keepdims=True)
    blend = contract(near_w.astype(BF16), near_values, ((1,), (0,)))
    half = len(parts) // 2
    for n, ref in enumerate((mine_ref, other_ref)):
        group = [w.astype(BF16) for w in weights[n * half : (n + 1) * half]]
        blend = blend + contract(
            jnp.concatenate(group, axis=1), ref[count : 2 * count, :], ((1,), (0,))
        )
    lane = lax.broadcasted_iota(jnp.int32, (HD, HD), 1)
    stats = jnp.where(lane < 64, shift, sums)
    for g in range(8):
        for node in (0, 8):
            at = 16 * g + node
            to = pl.ds(8 * node + g, 8, stride=8)
            blend_scr[to, :] = blend[at : at + 8]
            stat_scr[to, :] = stats[at : at + 8]
    for j in range(GROUP):
        out_ref[j, 0:16, :] = blend_scr[16 * j : 16 * j + 16, :].astype(BF16)
        out_ref[j, 16:32, :] = stat_scr[16 * j : 16 * j + 16, :].astype(BF16)


def retained_attend(width, summed, mine, other, ancestors):
    vmem = pl.BlockSpec(memory_space=pltpu.VMEM)
    return pl.pallas_call(
        functools.partial(retained_kernel, width),
        in_specs=[vmem, vmem, vmem, vmem],
        out_specs=vmem,
        out_shape=jax.ShapeDtypeStruct((GROUP, 32, HD), BF16),
        scratch_shapes=[pltpu.VMEM((HD, HD), F32), pltpu.VMEM((HD, HD), F32)],
        compiler_params=pltpu.CompilerParams(vmem_limit_bytes=8 << 20),
        name="retained_attend",
    )(summed, mine, other, ancestors)


def finish_kernel(parts_ref, out_ref):
    for h in range(2):
        sources = [2 * z + h for z in range(4)]
        stats = [parts_ref[a, 16:32, :].astype(F32) for a in sources]
        highest = stats[0]
        for stat in stats[1:]:
            highest = jnp.maximum(highest, stat)
        blend = None
        total = None
        for a, stat in zip(sources, stats):
            factor = jnp.exp2(stat[:, 0:1] - highest[:, 0:1])
            part = parts_ref[a, 0:16, :].astype(F32) * factor
            weight = stat[:, 64:65] * factor
            blend = part if blend is None else blend + part
            total = weight if total is None else total + weight
        heads = blend / total
        for i in range(2):
            for g in range(8):
                at = 8 * h + g
                out_ref[i : i + 1, at * HD : (at + 1) * HD] = heads[8 * i + g : 8 * i + g + 1]


def finish_upper(parts):
    return pl.pallas_call(
        finish_kernel,
        out_shape=jax.ShapeDtypeStruct((2, 16 * HD), F32),
        name="finish_upper",
    )(pltpu.with_memory_space_constraint(parts, pltpu.VMEM))


def swapped(array, axis):
    return lax.ppermute(array, axis, [(0, 1), (1, 0)])


def shards(
    tree_hidden,
    query_low,
    key_tree_low,
    value_tree_low,
    cache_keys,
    cache_values,
    cache_lengths,
    ancestors,
    out_weight,
    norm_gain,
    w_query_up,
    w_key_up,
    w_value_up,
    retained_keys,
    retained_values,
    retained_index,
):
    seq_count = lax.axis_size(SEQ)
    requests, cache_part, kv_heads, _ = cache_keys.shape
    kept = retained_keys.shape[1]
    width = tree_hidden.shape[1] * seq_count
    own_q = query_low.reshape(2, 2, 8, HD).transpose(1, 0, 2, 3).reshape(32, HD)
    kv_own = jnp.concatenate(
        [
            key_tree_low.reshape(2, 2, HD).transpose(1, 0, 2).reshape(4, HD),
            value_tree_low.reshape(2, 2, HD).transpose(1, 0, 2).reshape(4, HD),
        ],
        axis=0,
    )
    kept_own, kept_given = split_heads(
        cache_lengths,
        retained_keys.reshape(kept * kv_heads, HD),
        retained_values.reshape(kept * kv_heads, HD),
        retained_index[0].T,
    )
    kept_other = swapped(kept_given, "yh")
    queries = spread(spread(own_q, DEPTH).reshape(-1, HD), FACE).reshape(GROUP, GROUP, 32, HD)
    turned_keys = turn(cache_keys.reshape(requests, cache_part * kv_heads, HD))
    parts = cache_attend(
        cache_lengths,
        queries,
        turned_keys,
        cache_values.reshape(requests, cache_part * kv_heads, HD),
        kv_own,
    )
    folded = spread(fold_parts(exchanged(parts, FACE)), DEPTH)
    heads = merge_lower(folded, queries, ancestors)
    terms = output_terms(spread(heads, FACE), out_weight)
    terms = terms + swapped(terms, "c")
    terms = terms + swapped(terms, "yl")
    residual, projected = project(
        tree_hidden, terms, norm_gain.reshape(1, -1), w_query_up, w_key_up, w_value_up
    )
    summed = jnp.sum(exchanged(projected, FACE).astype(F32), axis=0).astype(BF16)
    shares = jnp.broadcast_to(summed.reshape(2, 1, 176, HD), (2, 4, 176, HD))
    arrived = exchanged(shares.reshape(GROUP, 176, HD), DEPTH)
    mine = jnp.sum(arrived.astype(F32), axis=0).astype(BF16)
    upper = retained_attend(width, mine, kept_own, kept_other, ancestors)
    upper_heads = finish_upper(exchanged(upper, TEAM))
    return (residual, upper_heads)


def solution(mesh):
    fine = Mesh(
        mesh.devices.reshape(4, 2, 4, 2, 2, 2), ("x", "zh", "zl", "yh", "yl", "c")
    )
    seq, tp = SEQ, ("yl", "c")
    return jax.shard_map(
        shards,
        mesh=fine,
        in_specs=(
            P(None, seq),
            P(seq, tp),
            P(seq, tp),
            P(seq, tp),
            P(None, seq, tp, None),
            P(None, seq, tp, None),
            P(),
            P(),
            P(tp, seq),
            P(seq),
            P(seq, tp),
            P(seq, tp),
            P(seq, tp),
            P(seq, None, tp, None),
            P(seq, None, tp, None),
            P(seq, None, tp),
        ),
        out_specs=(P(None, seq), P(seq, tp)),
        check_vma=False,
    )
```

```python
import functools

import jax
import jax.numpy as jnp
from jax import lax
from jax.experimental import pallas as pl
from jax.experimental.pallas import tpu as pltpu
from jax.sharding import Mesh, PartitionSpec as P

HD = 128
GROUP = 8
SCALE = HD ** (-0.5)
SCALE2 = SCALE * 1.4426950408889634
MASKED = -1e30
FLOOR = -1e20
EPS = 1e-05
F32 = jnp.float32
BF16 = jnp.bfloat16

SEQ = ("x", "zh", "z1", "z0", "yh")
TEAM = ("z1", "yh")
DEPTH = ("zh", "z1", "z0")
FACE = ("x", "yh")


def contract(a, b, dims):
    return lax.dot_general(a, b, (dims, ((), ())), preferred_element_type=F32)


def exchanged(blocks, axis):
    return lax.all_to_all(blocks, axis, split_axis=0, concat_axis=0, tiled=True)


def spread(array, axis, near=False):
    copies = jnp.broadcast_to(array, (lax.axis_size(axis), *array.shape))
    if near:
        copies = pltpu.with_memory_space_constraint(copies, pltpu.VMEM)
    return exchanged(copies, axis)


def head_halves(rows):
    parity = lax.broadcasted_iota(jnp.int32, (16, HD), 0) % 2
    even = (parity == 0).astype(F32).astype(BF16)
    odd = (parity == 1).astype(F32).astype(BF16)
    count = rows.shape[0] // 16
    tiles = rows.reshape(count, 16, HD)
    first = (tiles * even[None]).reshape(rows.shape)
    second = (tiles * odd[None]).reshape(rows.shape)
    return jnp.concatenate([first, second], axis=1)


def shift_of(maximum):
    return jnp.maximum(maximum, FLOOR).astype(BF16).astype(F32)


def turn_kernel(k_hbm, kt_hbm, k_buf, kt_buf, sems):
    requests, keys, _ = k_buf.shape
    step = 256

    def fetch(r):
        return pltpu.make_async_copy(k_hbm.at[r], k_buf.at[r], sems.at[0, r])

    def store(r):
        return pltpu.make_async_copy(kt_buf.at[r], kt_hbm.at[r], sems.at[1, r])

    for r in range(requests):
        fetch(r).start()
    for r in range(requests):
        fetch(r).wait()
        for c in range(0, keys, step):
            kt_buf[r, :, c : c + step] = k_buf[r, c : c + step, :].T
        store(r).start()
    for r in range(requests):
        store(r).wait()


def turn(keys):
    requests, count, _ = keys.shape
    return pl.pallas_call(
        turn_kernel,
        in_specs=[pl.BlockSpec(memory_space=pltpu.HBM)],
        out_specs=pl.BlockSpec(memory_space=pltpu.HBM),
        out_shape=pltpu.HBM((requests, HD, count), BF16),
        scratch_shapes=[
            pltpu.VMEM((requests, count, HD), BF16),
            pltpu.VMEM((requests, HD, count), BF16),
            pltpu.SemaphoreType.DMA((2, requests)),
        ],
        compiler_params=pltpu.CompilerParams(vmem_limit_bytes=12 << 20),
        name="turn",
    )(pltpu.with_memory_space_constraint(keys, pltpu.HBM))


def cache_kernel(
    len_ref, q_ref, kt_hbm, v_hbm, kv_ref, out_ref, first_scr, second_scr, k_buf, v_buf, sems
):
    requests, _, keys = k_buf.shape

    def fetch_keys(r):
        return pltpu.make_async_copy(kt_hbm.at[r], k_buf.at[r], sems.at[0, r])

    def fetch_values(r):
        return pltpu.make_async_copy(v_hbm.at[r], v_buf.at[r], sems.at[1, r])

    for r in range(requests):
        fetch_keys(r).start()
        fetch_values(r).start()
    start = lax.axis_index(SEQ) * (keys // 2)
    rows = 16 * GROUP
    step = 256
    kv_own = kv_ref[...].astype(F32)
    odd = lax.broadcasted_iota(jnp.int32, (rows, HD), 1) % 2 == 1
    lane = lax.broadcasted_iota(jnp.int32, (rows, HD), 1)
    kept = {}
    column = lax.broadcasted_iota(jnp.int32, (1, step), 1)
    first_head = (column % 2 == 0).astype(F32).astype(BF16)
    second_head = (column % 2 == 1).astype(F32).astype(BF16)

    def score(r, scr):
        def half(h):
            return jnp.concatenate(
                [
                    q_ref[2 * (r // 2) + j % 2, 4 * (r % 2) + j // 2, 16 * h : 16 * h + 16, :]
                    for j in range(GROUP)
                ],
                axis=0,
            )

        queries = jnp.concatenate([half(0), half(1)], axis=1)
        limit = 2 * (len_ref[r] - start)
        folded = None
        for c in range(0, keys, step):
            turned = k_buf[r, :, c : c + step]
            both = jnp.concatenate([turned * first_head, turned * second_head], axis=0)
            part = contract(queries, both, ((1,), (0,))) * SCALE2
            part = part + jnp.where(column + c < limit, 0.0, MASKED)
            scr[:, c : c + step] = part
            for d in range(0, step, HD):
                piece = part[:, d : d + HD]
                folded = piece if folded is None else jnp.maximum(folded, piece)
        return folded

    def blend(r, scr, folded):
        s0 = shift_of(jnp.max(jnp.where(odd, MASKED, folded), axis=1, keepdims=True))
        s1 = shift_of(jnp.max(jnp.where(odd, folded, MASKED), axis=1, keepdims=True))
        shift = jnp.where(odd, s1, s0)
        total = jnp.zeros((rows, HD), F32)
        mixed = jnp.zeros((rows, 2 * HD), F32)
        for c in range(0, keys, step):
            pieces = []
            for d in range(c, c + step, HD):
                w = jnp.exp2(scr[:, d : d + HD] - shift)
                total = total + w
                pieces.append(w.astype(BF16))
            mixed = mixed + contract(
                jnp.concatenate(pieces, axis=1),
                head_halves(v_buf[r, c : c + step, :]),
                ((1,), (0,)),
            )
        l0 = jnp.sum(jnp.where(odd, 0.0, total), axis=1, keepdims=True)
        l1 = jnp.sum(jnp.where(odd, total, 0.0), axis=1, keepdims=True)
        columns = jnp.where(
            lane < 2, jnp.where(lane == 0, s0, l0), jnp.where(lane == 2, s1, l1)
        )
        kept[r] = columns.T
        for h in range(2):
            at = 2 * (r // 2) + h
            low = 16 * GROUP * (r % 2)
            out_ref[at, low : low + rows, :] = mixed[:, h * HD : (h + 1) * HD].astype(BF16)
            if r % 2 == 1:
                tile = jnp.concatenate(
                    [
                        kept[r - 1][2 * h : 2 * h + 2],
                        kept[r][2 * h : 2 * h + 2],
                        kv_own[2 * h : 2 * h + 2],
                        kv_own[4 + 2 * h : 6 + 2 * h],
                        jnp.zeros((8, HD), F32),
                    ],
                    axis=0,
                )
                out_ref[at, 2 * rows : 2 * rows + 16, :] = tile.astype(BF16)

    scratch = (first_scr, second_scr)
    fetch_keys(0).wait()
    folded = score(0, scratch[0])
    for r in range(requests):
        if r + 1 < requests:
            fetch_keys(r + 1).wait()
        fetch_values(r).wait()
        ahead = score(r + 1, scratch[(r + 1) % 2]) if r + 1 < requests else None
        blend(r, scratch[r % 2], folded)
        folded = ahead


def cache_attend(lengths, queries, keys, values, kv_own):
    requests, _, count = keys.shape
    vmem = pl.BlockSpec(memory_space=pltpu.VMEM)
    return pl.pallas_call(
        cache_kernel,
        in_specs=[
            pl.BlockSpec(memory_space=pltpu.SMEM),
            vmem,
            pl.BlockSpec(memory_space=pltpu.HBM),
            pl.BlockSpec(memory_space=pltpu.HBM),
            vmem,
        ],
        out_specs=vmem,
        out_shape=jax.ShapeDtypeStruct((GROUP, 32 * GROUP + 16, HD), BF16),
        scratch_shapes=[
            pltpu.VMEM((16 * GROUP, count), F32),
            pltpu.VMEM((16 * GROUP, count), F32),
            pltpu.VMEM((requests, HD, count), BF16),
            pltpu.VMEM((requests, count, HD), BF16),
            pltpu.SemaphoreType.DMA((2, requests)),
        ],
        compiler_params=pltpu.CompilerParams(vmem_limit_bytes=20 << 20),
        name="cache_attend",
    )(
        lengths,
        queries,
        pltpu.with_memory_space_constraint(keys, pltpu.HBM),
        pltpu.with_memory_space_constraint(values, pltpu.HBM),
        kv_own,
    )


def folded_parts(parts_ref):
    stats = parts_ref[:, 256:272, :].astype(F32)
    highest = jnp.max(stats, axis=0)
    factor = jnp.exp2(jnp.minimum(stats - highest[None], 0.0))
    columns = factor.reshape(HD, HD).T
    blends, sums = [], []
    for r in range(2):
        mixed = None
        total = None
        for source in range(GROUP):
            at = 16 * source + 2 * r
            part = parts_ref[source, HD * r : HD * r + HD, :].astype(F32) * columns[:, at : at + 1]
            weight = stats[source, 2 * r + 1 : 2 * r + 2] * factor[source, 2 * r : 2 * r + 1]
            mixed = part if mixed is None else mixed + part
            total = weight if total is None else total + weight
        blends.append(mixed)
        sums.append(total)
    return stats, highest, blends, sums


def fold_kernel(parts_ref, out_ref):
    _, highest, blends, sums = folded_parts(parts_ref)
    out_ref[0:HD, :] = blends[0].astype(BF16)
    out_ref[HD : 2 * HD, :] = blends[1].astype(BF16)
    first = 2 * lax.axis_index("x")
    tree0 = parts_ref[first, 256:272, :].astype(F32)[4:8]
    tree1 = parts_ref[first + 1, 256:272, :].astype(F32)[4:8]
    tile = jnp.concatenate(
        [
            highest[0:1],
            sums[0],
            highest[2:3],
            sums[1],
            tree0,
            tree1,
            jnp.zeros((4, HD), F32),
        ],
        axis=0,
    )
    out_ref[2 * HD : 2 * HD + 16, :] = tile.astype(BF16)


def fold_parts(parts):
    return pl.pallas_call(
        fold_kernel,
        in_specs=[pl.BlockSpec(memory_space=pltpu.VMEM)],
        out_specs=pl.BlockSpec(memory_space=pltpu.VMEM),
        out_shape=jax.ShapeDtypeStruct(parts.shape[1:], BF16),
        compiler_params=pltpu.CompilerParams(vmem_limit_bytes=8 << 20),
        name="fold_parts",
    )(parts)


def merge_kernel(parts_ref, q_ref, anc_ref, out_ref, scr):
    x = lax.axis_index("x")
    head = lax.axis_index("yh")
    stats, highest, blends, sums = folded_parts(parts_ref)
    padding = jnp.zeros((HD - 4, HD), F32)
    turned = jnp.concatenate([highest[0:1], sums[0], highest[2:3], sums[1], padding], axis=0).T
    entry = lax.broadcasted_iota(jnp.int32, (16, 64), 1)
    inner = entry % 16 - 4
    is_key = (inner >= 0) & (inner < 8) & (inner % 4 < 2)
    node_of = (entry // 16) * 4 + (inner // 4) * 2 + inner % 4
    pick = (is_key & (node_of == lax.broadcasted_iota(jnp.int32, (16, 64), 0))).astype(F32)
    place = (
        lax.broadcasted_iota(jnp.int32, (HD, 16), 0) // 8
        == lax.broadcasted_iota(jnp.int32, (HD, 16), 1)
    ).astype(F32)
    for r in range(2):
        tree = stats[4 * r : 4 * r + 4].reshape(64, HD)
        values = pltpu.roll(tree, 62, 0).astype(BF16)
        queries = jnp.concatenate(
            [
                jnp.where(
                    head == 0,
                    q_ref[2 * x + j % 2, 4 * r + j // 2, 0:16, :].astype(F32),
                    q_ref[2 * x + j % 2, 4 * r + j // 2, 16:32, :].astype(F32),
                )
                for j in range(GROUP)
            ],
            axis=0,
        ).astype(BF16)
        ancestry = anc_ref[2 * x + r].astype(F32).astype(BF16)
        seen = contract(ancestry, pick.astype(BF16), ((1,), (0,))).astype(BF16)
        seen = contract(place.astype(BF16), seen, ((1,), (0,)))
        scores = contract(queries, tree.astype(BF16), ((1,), (1,))) * SCALE2
        scores = jnp.where(seen > 0.5, scores, MASKED)
        m_near = jnp.max(scores, axis=1, keepdims=True)
        w_near = jnp.where(seen > 0.5, jnp.exp2(scores - m_near), 0.0)
        l_near = jnp.sum(w_near, axis=1, keepdims=True)
        o_near = contract(w_near.astype(BF16), values, ((1,), (0,)))
        m_far = turned[:, 2 * r : 2 * r + 1]
        top = jnp.maximum(m_far, m_near)
        f_far = jnp.exp2(m_far - top)
        f_near = jnp.exp2(m_near - top)
        denominator = turned[:, 2 * r + 1 : 2 * r + 2] * f_far + l_near * f_near
        scr[HD * r : HD * r + HD, :] = (blends[r] * f_far + o_near * f_near) / denominator
    for g in range(8):
        out_ref[:, g * HD : (g + 1) * HD] = scr[pl.ds(g, 32, stride=8), :].astype(BF16)


def merge_lower(parts, queries, ancestors):
    return pl.pallas_call(
        merge_kernel,
        in_specs=[pl.BlockSpec(memory_space=pltpu.VMEM)] * 3,
        out_specs=pl.BlockSpec(memory_space=pltpu.VMEM),
        out_shape=jax.ShapeDtypeStruct((32, 8 * HD), BF16),
        scratch_shapes=[pltpu.VMEM((2 * HD, HD), F32)],
        compiler_params=pltpu.CompilerParams(vmem_limit_bytes=8 << 20),
        name="merge_lower",
    )(parts, queries, ancestors)


def output_kernel(heads_ref, weight_ref, out_ref):
    half = weight_ref.shape[0] // 2
    total = None
    for h in range(2):
        rows = jnp.concatenate([heads_ref[2 * x + h] for x in range(4)], axis=0)
        term = contract(rows, weight_ref[h * half : (h + 1) * half, :], ((1,), (0,)))
        total = term if total is None else total + term
    out_ref[...] = total


def output_terms(heads, weight):
    return pl.pallas_call(
        output_kernel,
        in_specs=[pl.BlockSpec(memory_space=pltpu.VMEM)] * 2,
        out_specs=pl.BlockSpec(memory_space=pltpu.VMEM),
        out_shape=jax.ShapeDtypeStruct((4 * heads.shape[1], weight.shape[1]), F32),
        compiler_params=pltpu.CompilerParams(vmem_limit_bytes=8 << 20),
        name="output_terms",
    )(heads, weight)


def project_kernel(hidden_ref, terms_ref, gain_ref, wq_ref, wk_ref, wv_ref, res_ref, out_ref):
    residual = hidden_ref[...].astype(F32) + terms_ref[...]
    res_ref[...] = residual
    square = jnp.sum(residual * residual, axis=1, keepdims=True)
    coarse = square.astype(BF16).astype(F32)
    lane = lax.broadcasted_iota(jnp.int32, residual.shape, 1)
    squares = jnp.where(lane < 64, coarse, square - coarse).astype(BF16)
    scaled = (residual * gain_ref[...]).astype(BF16)
    q = contract(scaled, wq_ref[...], ((1,), (0,))).astype(BF16)
    k = contract(scaled, wk_ref[...], ((1,), (0,))).astype(BF16)
    v = contract(scaled, wv_ref[...], ((1,), (0,))).astype(BF16)
    for h in range(2):
        blocks = [q[:, (8 * h + g) * HD : (8 * h + g + 1) * HD] for g in range(8)]
        blocks += [k[:, h * HD : (h + 1) * HD], v[:, h * HD : (h + 1) * HD], squares]
        for r in range(8):
            for b, block in enumerate(blocks):
                at = (r % 2) * 176 + 16 * b
                out_ref[2 * (r // 2) + h, at : at + 16, :] = block[16 * r : 16 * r + 16]


def project(hidden, terms, gain, wq, wk, wv):
    rows = hidden.shape[0]
    return pl.pallas_call(
        project_kernel,
        out_shape=(
            jax.ShapeDtypeStruct((rows, HD), F32),
            jax.ShapeDtypeStruct((GROUP, 352, HD), BF16),
        ),
        compiler_params=pltpu.CompilerParams(vmem_limit_bytes=8 << 20),
        name="project",
    )(hidden, terms, gain, wq, wk, wv)


def split_kernel(len_ref, k_ref, v_ref, pos_ref, mine_ref, give_ref):
    own = lax.axis_index("yh")
    length = len_ref[lax.axis_index(SEQ) // GROUP]
    row = lax.broadcasted_iota(jnp.int32, (2 * HD, 2 * HD), 0)
    col = lax.broadcasted_iota(jnp.int32, (2 * HD, 2 * HD), 1)
    source = 2 * (row % HD) + jnp.where(row < HD, own, 1 - own)
    pick = (col == source).astype(F32).astype(BF16)
    count = k_ref.shape[0] // 2
    for at, ref in ((0, k_ref), (count, v_ref)):
        for c in range(0, count, HD):
            pair = contract(pick, ref[2 * c : 2 * c + 2 * HD, :], ((1,), (0,))).astype(BF16)
            mine_ref[at + c : at + c + HD, :] = pair[0:HD]
            give_ref[at + c : at + c + HD, :] = pair[HD:]
    kept = (pos_ref[...] < length).astype(F32)
    rows0 = [kept[0:1, c : c + HD] for c in range(0, count, HD)]
    rows1 = [kept[1:2, c : c + HD] for c in range(0, count, HD)]
    rest = jnp.zeros((16 - len(rows0), HD), F32)
    limits0 = jnp.concatenate(rows0 + [rest], axis=0)
    limits1 = jnp.concatenate(rows1 + [rest], axis=0)
    mine_ref[2 * count : 2 * count + 16, :] = jnp.where(own == 0, limits0, limits1).astype(BF16)
    give_ref[2 * count : 2 * count + 16, :] = jnp.where(own == 0, limits1, limits0).astype(BF16)


def split_heads(lengths, keys, values, positions):
    count = keys.shape[0]
    vmem = pl.BlockSpec(memory_space=pltpu.VMEM)
    return pl.pallas_call(
        split_kernel,
        in_specs=[pl.BlockSpec(memory_space=pltpu.SMEM), vmem, vmem, vmem],
        out_specs=[vmem, vmem],
        out_shape=[jax.ShapeDtypeStruct((count + 16, HD), BF16)] * 2,
        compiler_params=pltpu.CompilerParams(vmem_limit_bytes=8 << 20),
        name="split_heads",
    )(lengths, keys, values, positions)


def retained_kernel(width, terms_ref, a_ref, b_ref, c_ref, d_ref, anc_ref, out_ref, blend_scr, stat_scr):
    kept_refs = (a_ref, b_ref, c_ref, d_ref)
    request = lax.axis_index(SEQ) // GROUP
    leader = lax.axis_index("z1") == 0
    raw = terms_ref[0].astype(F32)
    for z in range(1, GROUP):
        raw = raw + terms_ref[z].astype(F32)
    square = raw[160:176, 0:1] + raw[160:176, 64:65]
    inverse = lax.rsqrt(square / width + EPS)

    def up(b):
        return (raw[16 * b : 16 * b + 16] * inverse).astype(BF16)

    queries = jnp.concatenate([up(g) for g in range(8)], axis=0)
    near_keys, near_values = up(8), up(9)
    count = (a_ref.shape[0] - 16) // 2
    parts = []
    for ref in kept_refs:
        limits = ref[2 * count : 2 * count + 16, :].astype(F32)
        part = contract(queries, ref[0:count, :], ((1,), (1,))) * SCALE2
        for c in range(0, count, HD):
            usable = limits[c // HD : c // HD + 1] > 0.5
            parts.append(jnp.where(usable, part[:, c : c + HD], MASKED))
    row_pick = (
        lax.broadcasted_iota(jnp.int32, (HD, 16), 0) % 16
        == lax.broadcasted_iota(jnp.int32, (HD, 16), 1)
    )
    ancestry = anc_ref[request].astype(F32).astype(BF16)
    seen = contract(row_pick.astype(F32).astype(BF16), ancestry, ((1,), (0,)))
    close = contract(queries, near_keys, ((1,), (1,))) * SCALE2
    close = jnp.where((seen > 0.5) & leader, close, MASKED)
    folded = parts[0]
    for part in parts[1:]:
        folded = jnp.maximum(folded, part)
    top = jnp.maximum(
        jnp.max(folded, axis=1, keepdims=True), jnp.max(close, axis=1, keepdims=True)
    )
    shift = shift_of(top)
    weights = [jnp.exp2(part - shift) for part in parts]
    near_w = jnp.exp2(close - shift)
    total = weights[0]
    for w in weights[1:]:
        total = total + w
    sums = jnp.sum(total, axis=1, keepdims=True) + jnp.sum(near_w, axis=1, keepdims=True)
    blend = contract(near_w.astype(BF16), near_values, ((1,), (0,)))
    share = len(parts) // len(kept_refs)
    for n, ref in enumerate(kept_refs):
        group = [w.astype(BF16) for w in weights[n * share : (n + 1) * share]]
        blend = blend + contract(
            jnp.concatenate(group, axis=1), ref[count : 2 * count, :], ((1,), (0,))
        )
    lane = lax.broadcasted_iota(jnp.int32, (HD, HD), 1)
    stats = jnp.where(lane < 64, shift, sums)
    for g in range(8):
        for node in (0, 8):
            at = 16 * g + node
            to = pl.ds(8 * node + g, 8, stride=8)
            blend_scr[to, :] = blend[at : at + 8]
            stat_scr[to, :] = stats[at : at + 8]
    for j in range(4):
        member = (j // 2) * 4 + lax.axis_index("z0") * 2 + j % 2
        rows = pl.ds(pl.multiple_of(16 * member, 16), 16)
        out_ref[j, 0:16, :] = blend_scr[rows, :].astype(BF16)
        out_ref[j, 16:32, :] = stat_scr[rows, :].astype(BF16)


def retained_attend(width, terms, kept, ancestors):
    vmem = pl.BlockSpec(memory_space=pltpu.VMEM)
    return pl.pallas_call(
        functools.partial(retained_kernel, width),
        in_specs=[vmem] * (2 + len(kept)),
        out_specs=vmem,
        out_shape=jax.ShapeDtypeStruct((4, 32, HD), BF16),
        scratch_shapes=[pltpu.VMEM((HD, HD), F32), pltpu.VMEM((HD, HD), F32)],
        compiler_params=pltpu.CompilerParams(vmem_limit_bytes=8 << 20),
        name="retained_attend",
    )(terms, *kept, ancestors)


def finish_kernel(parts_ref, out_ref):
    for h in range(2):
        sources = [2 * z + h for z in range(2)]
        stats = [parts_ref[a, 16:32, :].astype(F32) for a in sources]
        highest = stats[0]
        for stat in stats[1:]:
            highest = jnp.maximum(highest, stat)
        blend = None
        total = None
        for a, stat in zip(sources, stats):
            factor = jnp.exp2(stat[:, 0:1] - highest[:, 0:1])
            part = parts_ref[a, 0:16, :].astype(F32) * factor
            weight = stat[:, 64:65] * factor
            blend = part if blend is None else blend + part
            total = weight if total is None else total + weight
        heads = blend / total
        for i in range(2):
            for g in range(8):
                at = 8 * h + g
                out_ref[i : i + 1, at * HD : (at + 1) * HD] = heads[8 * i + g : 8 * i + g + 1]


def finish_upper(parts):
    return pl.pallas_call(
        finish_kernel,
        out_shape=jax.ShapeDtypeStruct((2, 16 * HD), F32),
        name="finish_upper",
    )(pltpu.with_memory_space_constraint(parts, pltpu.VMEM))


def swapped(array, axis):
    last = lax.axis_size(axis) - 1
    return lax.ppermute(array, axis, [(i, last - i) for i in range(last + 1)])


def shards(
    tree_hidden,
    query_low,
    key_tree_low,
    value_tree_low,
    cache_keys,
    cache_values,
    cache_lengths,
    ancestors,
    out_weight,
    norm_gain,
    w_query_up,
    w_key_up,
    w_value_up,
    retained_keys,
    retained_values,
    retained_index,
):
    seq_count = lax.axis_size(SEQ)
    requests, cache_part, kv_heads, _ = cache_keys.shape
    kept = retained_keys.shape[1]
    width = tree_hidden.shape[1] * seq_count
    own_q = query_low.reshape(2, 2, 8, HD).transpose(1, 0, 2, 3).reshape(32, HD)
    kv_own = jnp.concatenate(
        [
            key_tree_low.reshape(2, 2, HD).transpose(1, 0, 2).reshape(4, HD),
            value_tree_low.reshape(2, 2, HD).transpose(1, 0, 2).reshape(4, HD),
        ],
        axis=0,
    )
    kept_own, kept_given = split_heads(
        cache_lengths,
        retained_keys.reshape(kept * kv_heads, HD),
        retained_values.reshape(kept * kv_heads, HD),
        retained_index[0].T,
    )
    queries = spread(spread(own_q, DEPTH), FACE, True)
    turned_keys = turn(cache_keys.reshape(requests, cache_part * kv_heads, HD))
    parts = cache_attend(
        cache_lengths,
        queries,
        turned_keys,
        cache_values.reshape(requests, cache_part * kv_heads, HD),
        kv_own,
    )
    folded = spread(fold_parts(exchanged(parts, FACE)), DEPTH)
    heads = merge_lower(folded, queries, ancestors)
    terms = output_terms(spread(heads, FACE), out_weight)
    terms = terms + swapped(terms, "c")
    terms = terms + swapped(terms, "yl")
    residual, projected = project(
        tree_hidden, terms, norm_gain.reshape(1, -1), w_query_up, w_key_up, w_value_up
    )
    summed = jnp.sum(exchanged(projected, FACE).astype(F32), axis=0).astype(BF16)
    held = (
        kept_own,
        swapped(kept_given, "yh"),
        swapped(kept_own, "z0"),
        swapped(kept_given, ("z0", "yh")),
    )
    summed, held = lax.optimization_barrier((summed, held))
    shares = jnp.broadcast_to(summed.reshape(2, 1, 176, HD), (2, 4, 176, HD))
    arrived = exchanged(shares.reshape(GROUP, 176, HD), DEPTH)
    upper = retained_attend(width, arrived, held, ancestors)
    upper_heads = finish_upper(exchanged(upper, TEAM))
    return (residual, upper_heads)


def solution(mesh):
    fine = Mesh(
        mesh.devices.reshape(4, 2, 2, 2, 2, 2, 2),
        ("x", "zh", "z1", "z0", "yh", "yl", "c"),
    )
    seq, tp = SEQ, ("yl", "c")
    return jax.shard_map(
        shards,
        mesh=fine,
        in_specs=(
            P(None, seq),
            P(seq, tp),
            P(seq, tp),
            P(seq, tp),
            P(None, seq, tp, None),
            P(None, seq, tp, None),
            P(),
            P(),
            P(tp, seq),
            P(seq),
            P(seq, tp),
            P(seq, tp),
            P(seq, tp),
            P(seq, None, tp, None),
            P(seq, None, tp, None),
            P(seq, None, tp),
        ),
        out_specs=(P(None, seq), P(seq, tp)),
        check_vma=False,
    )
```

```python
import functools

import jax
import jax.numpy as jnp
from jax import lax
from jax.experimental import pallas as pl
from jax.experimental.pallas import tpu as pltpu
from jax.sharding import Mesh, PartitionSpec as P

HD = 128
GROUP = 8
SCALE = HD ** (-0.5)
SCALE2 = SCALE * 1.4426950408889634
MASKED = -1e30
FLOOR = -1e20
EPS = 1e-05
F32 = jnp.float32
BF16 = jnp.bfloat16

SEQ = ("x", "zh", "zl", "yh")
TEAM = ("zl", "yh")
DEPTH = ("zh", "zl")
FACE = ("x", "yh")


def contract(a, b, dims):
    return lax.dot_general(a, b, (dims, ((), ())), preferred_element_type=F32)


def exchanged(blocks, axis):
    return lax.all_to_all(blocks, axis, split_axis=0, concat_axis=0, tiled=True)


def spread(array, axis, near=False):
    copies = jnp.broadcast_to(array, (lax.axis_size(axis), *array.shape))
    if near:
        copies = pltpu.with_memory_space_constraint(copies, pltpu.VMEM)
    return exchanged(copies, axis)


def head_halves(rows):
    parity = lax.broadcasted_iota(jnp.int32, (16, HD), 0) % 2
    even = (parity == 0).astype(F32).astype(BF16)
    odd = (parity == 1).astype(F32).astype(BF16)
    count = rows.shape[0] // 16
    tiles = rows.reshape(count, 16, HD)
    first = (tiles * even[None]).reshape(rows.shape)
    second = (tiles * odd[None]).reshape(rows.shape)
    return jnp.concatenate([first, second], axis=1)


def shift_of(maximum):
    return jnp.maximum(maximum, FLOOR).astype(BF16).astype(F32)


def turn_kernel(k_hbm, kt_hbm, k_buf, kt_buf, sems):
    requests, keys, _ = k_buf.shape
    step = 256

    def fetch(r):
        return pltpu.make_async_copy(k_hbm.at[r], k_buf.at[r], sems.at[0, r])

    def store(r):
        return pltpu.make_async_copy(kt_buf.at[r], kt_hbm.at[r], sems.at[1, r])

    for r in range(requests):
        fetch(r).start()
    for r in range(requests):
        fetch(r).wait()
        for c in range(0, keys, step):
            kt_buf[r, :, c : c + step] = k_buf[r, c : c + step, :].T
        store(r).start()
    for r in range(requests):
        store(r).wait()


def turn(keys):
    requests, count, _ = keys.shape
    return pl.pallas_call(
        turn_kernel,
        in_specs=[pl.BlockSpec(memory_space=pltpu.HBM)],
        out_specs=pl.BlockSpec(memory_space=pltpu.HBM),
        out_shape=pltpu.HBM((requests, HD, count), BF16),
        scratch_shapes=[
            pltpu.VMEM((requests, count, HD), BF16),
            pltpu.VMEM((requests, HD, count), BF16),
            pltpu.SemaphoreType.DMA((2, requests)),
        ],
        compiler_params=pltpu.CompilerParams(vmem_limit_bytes=12 << 20),
        name="turn",
    )(pltpu.with_memory_space_constraint(keys, pltpu.HBM))


def cache_kernel(
    len_ref, q_ref, kt_hbm, v_hbm, kv_ref, out_ref, first_scr, second_scr, k_buf, v_buf, sems
):
    requests, _, keys = k_buf.shape

    def fetch_keys(r):
        return pltpu.make_async_copy(kt_hbm.at[r], k_buf.at[r], sems.at[0, r])

    def fetch_values(r):
        return pltpu.make_async_copy(v_hbm.at[r], v_buf.at[r], sems.at[1, r])

    for r in range(requests):
        fetch_keys(r).start()
        fetch_values(r).start()
    start = lax.axis_index(SEQ) * (keys // 2)
    rows = 16 * GROUP
    step = 256
    kv_own = kv_ref[...].astype(F32)
    odd = lax.broadcasted_iota(jnp.int32, (rows, HD), 1) % 2 == 1
    lane = lax.broadcasted_iota(jnp.int32, (rows, HD), 1)
    kept = {}
    column = lax.broadcasted_iota(jnp.int32, (1, step), 1)
    first_head = (column % 2 == 0).astype(F32).astype(BF16)
    second_head = (column % 2 == 1).astype(F32).astype(BF16)

    def score(r, scr):
        def half(h):
            return jnp.concatenate(
                [
                    q_ref[2 * (r // 2) + j % 2, 4 * (r % 2) + j // 2, 16 * h : 16 * h + 16, :]
                    for j in range(GROUP)
                ],
                axis=0,
            )

        queries = jnp.concatenate([half(0), half(1)], axis=1)
        limit = 2 * (len_ref[r] - start)
        folded = None
        for c in range(0, keys, step):
            turned = k_buf[r, :, c : c + step]
            both = jnp.concatenate([turned * first_head, turned * second_head], axis=0)
            part = contract(queries, both, ((1,), (0,))) * SCALE2
            part = part + jnp.where(column + c < limit, 0.0, MASKED)
            scr[:, c : c + step] = part
            for d in range(0, step, HD):
                piece = part[:, d : d + HD]
                folded = piece if folded is None else jnp.maximum(folded, piece)
        return folded

    def blend(r, scr, folded):
        s0 = shift_of(jnp.max(jnp.where(odd, MASKED, folded), axis=1, keepdims=True))
        s1 = shift_of(jnp.max(jnp.where(odd, folded, MASKED), axis=1, keepdims=True))
        shift = jnp.where(odd, s1, s0)
        total = jnp.zeros((rows, HD), F32)
        mixed = jnp.zeros((rows, 2 * HD), F32)
        for c in range(0, keys, step):
            pieces = []
            for d in range(c, c + step, HD):
                w = jnp.exp2(scr[:, d : d + HD] - shift)
                total = total + w
                pieces.append(w.astype(BF16))
            mixed = mixed + contract(
                jnp.concatenate(pieces, axis=1),
                head_halves(v_buf[r, c : c + step, :]),
                ((1,), (0,)),
            )
        l0 = jnp.sum(jnp.where(odd, 0.0, total), axis=1, keepdims=True)
        l1 = jnp.sum(jnp.where(odd, total, 0.0), axis=1, keepdims=True)
        columns = jnp.where(
            lane < 2, jnp.where(lane == 0, s0, l0), jnp.where(lane == 2, s1, l1)
        )
        kept[r] = columns.T
        for h in range(2):
            at = 2 * (r // 2) + h
            low = 16 * GROUP * (r % 2)
            out_ref[at, low : low + rows, :] = mixed[:, h * HD : (h + 1) * HD].astype(BF16)
            if r % 2 == 1:
                tile = jnp.concatenate(
                    [
                        kept[r - 1][2 * h : 2 * h + 2],
                        kept[r][2 * h : 2 * h + 2],
                        kv_own[2 * h : 2 * h + 2],
                        kv_own[4 + 2 * h : 6 + 2 * h],
                        jnp.zeros((8, HD), F32),
                    ],
                    axis=0,
                )
                out_ref[at, 2 * rows : 2 * rows + 16, :] = tile.astype(BF16)

    scratch = (first_scr, second_scr)
    fetch_keys(0).wait()
    folded = score(0, scratch[0])
    for r in range(requests):
        if r + 1 < requests:
            fetch_keys(r + 1).wait()
        fetch_values(r).wait()
        ahead = score(r + 1, scratch[(r + 1) % 2]) if r + 1 < requests else None
        blend(r, scratch[r % 2], folded)
        folded = ahead


def cache_attend(lengths, queries, keys, values, kv_own):
    requests, _, count = keys.shape
    vmem = pl.BlockSpec(memory_space=pltpu.VMEM)
    return pl.pallas_call(
        cache_kernel,
        in_specs=[
            pl.BlockSpec(memory_space=pltpu.SMEM),
            vmem,
            pl.BlockSpec(memory_space=pltpu.HBM),
            pl.BlockSpec(memory_space=pltpu.HBM),
            vmem,
        ],
        out_specs=vmem,
        out_shape=jax.ShapeDtypeStruct((GROUP, 32 * GROUP + 16, HD), BF16),
        scratch_shapes=[
            pltpu.VMEM((16 * GROUP, count), F32),
            pltpu.VMEM((16 * GROUP, count), F32),
            pltpu.VMEM((requests, HD, count), BF16),
            pltpu.VMEM((requests, count, HD), BF16),
            pltpu.SemaphoreType.DMA((2, requests)),
        ],
        compiler_params=pltpu.CompilerParams(vmem_limit_bytes=20 << 20),
        name="cache_attend",
    )(
        lengths,
        queries,
        pltpu.with_memory_space_constraint(keys, pltpu.HBM),
        pltpu.with_memory_space_constraint(values, pltpu.HBM),
        kv_own,
    )


def folded_parts(parts_ref):
    stats = parts_ref[:, 256:272, :].astype(F32)
    highest = jnp.max(stats, axis=0)
    factor = jnp.exp2(jnp.minimum(stats - highest[None], 0.0))
    columns = factor.reshape(HD, HD).T
    blends, sums = [], []
    for r in range(2):
        mixed = None
        total = None
        for source in range(GROUP):
            at = 16 * source + 2 * r
            part = parts_ref[source, HD * r : HD * r + HD, :].astype(F32) * columns[:, at : at + 1]
            weight = stats[source, 2 * r + 1 : 2 * r + 2] * factor[source, 2 * r : 2 * r + 1]
            mixed = part if mixed is None else mixed + part
            total = weight if total is None else total + weight
        blends.append(mixed)
        sums.append(total)
    return stats, highest, blends, sums


def fold_kernel(parts_ref, out_ref):
    _, highest, blends, sums = folded_parts(parts_ref)
    out_ref[0:HD, :] = blends[0].astype(BF16)
    out_ref[HD : 2 * HD, :] = blends[1].astype(BF16)
    first = 2 * lax.axis_index("x")
    tree0 = parts_ref[first, 256:272, :].astype(F32)[4:8]
    tree1 = parts_ref[first + 1, 256:272, :].astype(F32)[4:8]
    tile = jnp.concatenate(
        [
            highest[0:1],
            sums[0],
            highest[2:3],
            sums[1],
            tree0,
            tree1,
            jnp.zeros((4, HD), F32),
        ],
        axis=0,
    )
    out_ref[2 * HD : 2 * HD + 16, :] = tile.astype(BF16)


def fold_parts(parts):
    return pl.pallas_call(
        fold_kernel,
        in_specs=[pl.BlockSpec(memory_space=pltpu.VMEM)],
        out_specs=pl.BlockSpec(memory_space=pltpu.VMEM),
        out_shape=jax.ShapeDtypeStruct(parts.shape[1:], BF16),
        compiler_params=pltpu.CompilerParams(vmem_limit_bytes=8 << 20),
        name="fold_parts",
    )(parts)


def merge_kernel(parts_ref, q_ref, anc_ref, out_ref, scr):
    x = lax.axis_index("x")
    own_rows = pl.ds(pl.multiple_of(16 * lax.axis_index("yh"), 16), 16)
    stats, highest, blends, sums = folded_parts(parts_ref)
    padding = jnp.zeros((HD - 4, HD), F32)
    turned = jnp.concatenate([highest[0:1], sums[0], highest[2:3], sums[1], padding], axis=0).T
    entry = lax.broadcasted_iota(jnp.int32, (16, 64), 1)
    inner = entry % 16 - 4
    is_key = (inner >= 0) & (inner < 8) & (inner % 4 < 2)
    node_of = (entry // 16) * 4 + (inner // 4) * 2 + inner % 4
    pick = (is_key & (node_of == lax.broadcasted_iota(jnp.int32, (16, 64), 0))).astype(F32)
    place = (
        lax.broadcasted_iota(jnp.int32, (HD, 16), 0) // 8
        == lax.broadcasted_iota(jnp.int32, (HD, 16), 1)
    ).astype(F32)
    for r in range(2):
        tree = stats[4 * r : 4 * r + 4].reshape(64, HD)
        values = pltpu.roll(tree, 62, 0).astype(BF16)
        queries = jnp.concatenate(
            [
                q_ref[2 * x + j % 2, 4 * r + j // 2, own_rows, :]
                for j in range(GROUP)
            ],
            axis=0,
        )
        ancestry = anc_ref[2 * x + r].astype(F32).astype(BF16)
        seen = contract(ancestry, pick.astype(BF16), ((1,), (0,))).astype(BF16)
        seen = contract(place.astype(BF16), seen, ((1,), (0,)))
        scores = contract(queries, tree.astype(BF16), ((1,), (1,))) * SCALE2
        scores = jnp.where(seen > 0.5, scores, MASKED)
        m_near = jnp.max(scores, axis=1, keepdims=True)
        w_near = jnp.where(seen > 0.5, jnp.exp2(scores - m_near), 0.0)
        l_near = jnp.sum(w_near, axis=1, keepdims=True)
        o_near = contract(w_near.astype(BF16), values, ((1,), (0,)))
        m_far = turned[:, 2 * r : 2 * r + 1]
        top = jnp.maximum(m_far, m_near)
        f_far = jnp.exp2(m_far - top)
        f_near = jnp.exp2(m_near - top)
        denominator = turned[:, 2 * r + 1 : 2 * r + 2] * f_far + l_near * f_near
        scr[HD * r : HD * r + HD, :] = (blends[r] * f_far + o_near * f_near) / denominator
    for g in range(8):
        out_ref[:, g * HD : (g + 1) * HD] = scr[pl.ds(g, 32, stride=8), :].astype(BF16)


def merge_lower(parts, queries, ancestors):
    return pl.pallas_call(
        merge_kernel,
        in_specs=[pl.BlockSpec(memory_space=pltpu.VMEM)] * 3,
        out_specs=pl.BlockSpec(memory_space=pltpu.VMEM),
        out_shape=jax.ShapeDtypeStruct((32, 8 * HD), BF16),
        scratch_shapes=[pltpu.VMEM((2 * HD, HD), F32)],
        compiler_params=pltpu.CompilerParams(vmem_limit_bytes=8 << 20),
        name="merge_lower",
    )(parts, queries, ancestors)


def output_kernel(heads_ref, weight_ref, out_ref):
    half = weight_ref.shape[0] // 2
    total = None
    for h in range(2):
        rows = jnp.concatenate([heads_ref[2 * x + h] for x in range(4)], axis=0)
        term = contract(rows, weight_ref[h * half : (h + 1) * half, :], ((1,), (0,)))
        total = term if total is None else total + term
    out_ref[...] = total


def output_terms(heads, weight):
    return pl.pallas_call(
        output_kernel,
        in_specs=[pl.BlockSpec(memory_space=pltpu.VMEM)] * 2,
        out_specs=pl.BlockSpec(memory_space=pltpu.VMEM),
        out_shape=jax.ShapeDtypeStruct((4 * heads.shape[1], weight.shape[1]), F32),
        compiler_params=pltpu.CompilerParams(vmem_limit_bytes=8 << 20),
        name="output_terms",
    )(heads, weight)


def project_kernel(hidden_ref, terms_ref, gain_ref, wq_ref, wk_ref, wv_ref, res_ref, out_ref):
    residual = hidden_ref[...].astype(F32) + terms_ref[...]
    res_ref[...] = residual
    square = jnp.sum(residual * residual, axis=1, keepdims=True)
    coarse = square.astype(BF16).astype(F32)
    fine = square - coarse
    lane = lax.broadcasted_iota(jnp.int32, (8, HD), 1)
    scaled = (residual * gain_ref[...]).astype(BF16)
    q = contract(scaled, wq_ref[...], ((1,), (0,))).astype(BF16)
    k = contract(scaled, wk_ref[...], ((1,), (0,))).astype(BF16)
    v = contract(scaled, wv_ref[...], ((1,), (0,))).astype(BF16)
    for h in range(2):
        blocks = [q[:, (8 * h + g) * HD : (8 * h + g + 1) * HD] for g in range(8)]
        blocks += [k[:, h * HD : (h + 1) * HD], v[:, h * HD : (h + 1) * HD]]
        for r in range(8):
            at = (r % 2) * 168
            dest = 2 * (r // 2) + h
            for b, block in enumerate(blocks):
                out_ref[dest, at + 16 * b : at + 16 * b + 16, :] = block[16 * r : 16 * r + 16]
            low, high = slice(16 * r, 16 * r + 8), slice(16 * r + 8, 16 * r + 16)
            squares = jnp.where(
                lane < 64,
                jnp.where(lane < 32, coarse[low], fine[low]),
                jnp.where(lane < 96, coarse[high], fine[high]),
            )
            out_ref[dest, at + 160 : at + 168, :] = squares.astype(BF16)


def project(hidden, terms, gain, wq, wk, wv):
    rows = hidden.shape[0]
    return pl.pallas_call(
        project_kernel,
        out_shape=(
            jax.ShapeDtypeStruct((rows, HD), F32),
            jax.ShapeDtypeStruct((GROUP, 336, HD), BF16),
        ),
        compiler_params=pltpu.CompilerParams(vmem_limit_bytes=8 << 20),
        name="project",
    )(hidden, terms, gain, wq, wk, wv)


def split_kernel(len_ref, k_ref, v_ref, pos_ref, mine_ref, give_ref):
    own = lax.axis_index("yh")
    length = len_ref[lax.axis_index(SEQ) // GROUP]
    row = lax.broadcasted_iota(jnp.int32, (2 * HD, 2 * HD), 0)
    col = lax.broadcasted_iota(jnp.int32, (2 * HD, 2 * HD), 1)
    source = 2 * (row % HD) + jnp.where(row < HD, own, 1 - own)
    pick = (col == source).astype(F32).astype(BF16)
    count = k_ref.shape[0] // 2
    for at, ref in ((0, k_ref), (count, v_ref)):
        for c in range(0, count, HD):
            pair = contract(pick, ref[2 * c : 2 * c + 2 * HD, :], ((1,), (0,))).astype(BF16)
            mine_ref[at + c : at + c + HD, :] = pair[0:HD]
            give_ref[at + c : at + c + HD, :] = pair[HD:]
    kept = (pos_ref[...] < length).astype(F32)
    rows0 = [kept[0:1, c : c + HD] for c in range(0, count, HD)]
    rows1 = [kept[1:2, c : c + HD] for c in range(0, count, HD)]
    rest = jnp.zeros((16 - len(rows0), HD), F32)
    limits0 = jnp.concatenate(rows0 + [rest], axis=0)
    limits1 = jnp.concatenate(rows1 + [rest], axis=0)
    mine_ref[2 * count : 2 * count + 16, :] = jnp.where(own == 0, limits0, limits1).astype(BF16)
    give_ref[2 * count : 2 * count + 16, :] = jnp.where(own == 0, limits1, limits0).astype(BF16)


def split_heads(lengths, keys, values, positions):
    count = keys.shape[0]
    vmem = pl.BlockSpec(memory_space=pltpu.VMEM)
    return pl.pallas_call(
        split_kernel,
        in_specs=[pl.BlockSpec(memory_space=pltpu.SMEM), vmem, vmem, vmem],
        out_specs=[vmem, vmem],
        out_shape=[jax.ShapeDtypeStruct((count + 16, HD), BF16)] * 2,
        compiler_params=pltpu.CompilerParams(vmem_limit_bytes=8 << 20),
        name="split_heads",
    )(lengths, keys, values, positions)


def retained_kernel(width, terms_ref, mine_ref, other_ref, anc_ref, out_ref, blend_scr, stat_scr):
    request = lax.axis_index(SEQ) // GROUP
    leader = lax.axis_index("zl") == 0
    raw = terms_ref[0].astype(F32)
    for z in range(1, GROUP):
        raw = raw + terms_ref[z].astype(F32)
    tile = raw[160:168]
    square = jnp.concatenate(
        [tile[:, 0:1] + tile[:, 32:33], tile[:, 64:65] + tile[:, 96:97]], axis=0
    )
    inverse = lax.rsqrt(square / width + EPS)

    def up(b):
        return (raw[16 * b : 16 * b + 16] * inverse).astype(BF16)

    queries = jnp.concatenate([up(g) for g in range(8)], axis=0)
    near_keys, near_values = up(8), up(9)
    count = (mine_ref.shape[0] - 16) // 2
    parts = []
    for ref in (mine_ref, other_ref):
        limits = ref[2 * count : 2 * count + 16, :].astype(F32)
        part = contract(queries, ref[0:count, :], ((1,), (1,))) * SCALE2
        for c in range(0, count, HD):
            usable = limits[c // HD : c // HD + 1] > 0.5
            parts.append(jnp.where(usable, part[:, c : c + HD], MASKED))
    row_pick = (
        lax.broadcasted_iota(jnp.int32, (HD, 16), 0) % 16
        == lax.broadcasted_iota(jnp.int32, (HD, 16), 1)
    )
    ancestry = anc_ref[request].astype(F32).astype(BF16)
    seen = contract(row_pick.astype(F32).astype(BF16), ancestry, ((1,), (0,)))
    close = contract(queries, near_keys, ((1,), (1,))) * SCALE2
    close = jnp.where((seen > 0.5) & leader, close, MASKED)
    folded = parts[0]
    for part in parts[1:]:
        folded = jnp.maximum(folded, part)
    top = jnp.maximum(
        jnp.max(folded, axis=1, keepdims=True), jnp.max(close, axis=1, keepdims=True)
    )
    shift = shift_of(top)
    weights = [jnp.exp2(part - shift) for part in parts]
    near_w = jnp.exp2(close - shift)
    total = weights[0]
    for w in weights[1:]:
        total = total + w
    sums = jnp.sum(total, axis=1, keepdims=True) + jnp.sum(near_w, axis=1, keepdims=True)
    blend = contract(near_w.astype(BF16), near_values, ((1,), (0,)))
    half = len(parts) // 2
    for n, ref in enumerate((mine_ref, other_ref)):
        group = [w.astype(BF16) for w in weights[n * half : (n + 1) * half]]
        blend = blend + contract(
            jnp.concatenate(group, axis=1), ref[count : 2 * count, :], ((1,), (0,))
        )
    lane = lax.broadcasted_iota(jnp.int32, (HD, HD), 1)
    stats = jnp.where(lane < 64, shift, sums)
    for g in range(8):
        for node in (0, 8):
            at = 16 * g + node
            to = pl.ds(8 * node + g, 8, stride=8)
            blend_scr[to, :] = blend[at : at + 8]
            stat_scr[to, :] = stats[at : at + 8]
    for j in range(GROUP):
        out_ref[j, 0:16, :] = blend_scr[16 * j : 16 * j + 16, :].astype(BF16)
        out_ref[j, 16:32, :] = stat_scr[16 * j : 16 * j + 16, :].astype(BF16)


def retained_attend(width, terms, mine, other, ancestors):
    vmem = pl.BlockSpec(memory_space=pltpu.VMEM)
    return pl.pallas_call(
        functools.partial(retained_kernel, width),
        in_specs=[vmem, vmem, vmem, vmem],
        out_specs=vmem,
        out_shape=jax.ShapeDtypeStruct((GROUP, 32, HD), BF16),
        scratch_shapes=[pltpu.VMEM((HD, HD), F32), pltpu.VMEM((HD, HD), F32)],
        compiler_params=pltpu.CompilerParams(vmem_limit_bytes=8 << 20),
        name="retained_attend",
    )(terms, mine, other, ancestors)


def finish_kernel(parts_ref, out_ref):
    for h in range(2):
        sources = [2 * z + h for z in range(4)]
        stats = [parts_ref[a, 16:32, :].astype(F32) for a in sources]
        highest = stats[0]
        for stat in stats[1:]:
            highest = jnp.maximum(highest, stat)
        blend = None
        total = None
        for a, stat in zip(sources, stats):
            factor = jnp.exp2(stat[:, 0:1] - highest[:, 0:1])
            part = parts_ref[a, 0:16, :].astype(F32) * factor
            weight = stat[:, 64:65] * factor
            blend = part if blend is None else blend + part
            total = weight if total is None else total + weight
        heads = blend / total
        for i in range(2):
            for g in range(8):
                at = 8 * h + g
                out_ref[i : i + 1, at * HD : (at + 1) * HD] = heads[8 * i + g : 8 * i + g + 1]


def finish_upper(parts):
    return pl.pallas_call(
        finish_kernel,
        out_shape=jax.ShapeDtypeStruct((2, 16 * HD), F32),
        name="finish_upper",
    )(pltpu.with_memory_space_constraint(parts, pltpu.VMEM))


def swapped(array, axis):
    return lax.ppermute(array, axis, [(0, 1), (1, 0)])


def shards(
    tree_hidden,
    query_low,
    key_tree_low,
    value_tree_low,
    cache_keys,
    cache_values,
    cache_lengths,
    ancestors,
    out_weight,
    norm_gain,
    w_query_up,
    w_key_up,
    w_value_up,
    retained_keys,
    retained_values,
    retained_index,
):
    seq_count = lax.axis_size(SEQ)
    requests, cache_part, kv_heads, _ = cache_keys.shape
    kept = retained_keys.shape[1]
    width = tree_hidden.shape[1] * seq_count
    own_q = query_low.reshape(2, 2, 8, HD).transpose(1, 0, 2, 3).reshape(32, HD)
    kv_own = jnp.concatenate(
        [
            key_tree_low.reshape(2, 2, HD).transpose(1, 0, 2).reshape(4, HD),
            value_tree_low.reshape(2, 2, HD).transpose(1, 0, 2).reshape(4, HD),
        ],
        axis=0,
    )
    kept_own, kept_given = split_heads(
        cache_lengths,
        retained_keys.reshape(kept * kv_heads, HD),
        retained_values.reshape(kept * kv_heads, HD),
        retained_index[0].T,
    )
    kept_other = swapped(kept_given, "yh")
    queries = spread(spread(own_q, DEPTH), FACE, True)
    turned_keys = turn(cache_keys.reshape(requests, cache_part * kv_heads, HD))
    parts = cache_attend(
        cache_lengths,
        queries,
        turned_keys,
        cache_values.reshape(requests, cache_part * kv_heads, HD),
        kv_own,
    )
    folded = spread(fold_parts(exchanged(parts, FACE)), DEPTH)
    heads = merge_lower(folded, queries, ancestors)
    terms = output_terms(spread(heads, FACE), out_weight)
    terms = terms + swapped(terms, "c")
    terms = terms + swapped(terms, "yl")
    residual, projected = project(
        tree_hidden, terms, norm_gain.reshape(1, -1), w_query_up, w_key_up, w_value_up
    )
    summed = jnp.sum(exchanged(projected, FACE).astype(F32), axis=0).astype(BF16)
    shares = jnp.broadcast_to(summed.reshape(2, 1, 168, HD), (2, 4, 168, HD))
    shares = pltpu.with_memory_space_constraint(shares.reshape(GROUP, 168, HD), pltpu.VMEM)
    arrived = exchanged(shares, DEPTH)
    upper = retained_attend(width, arrived, kept_own, kept_other, ancestors)
    upper_heads = finish_upper(exchanged(upper, TEAM))
    return (residual, upper_heads)


def solution(mesh):
    fine = Mesh(
        mesh.devices.reshape(4, 2, 4, 2, 2, 2), ("x", "zh", "zl", "yh", "yl", "c")
    )
    seq, tp = SEQ, ("yl", "c")
    return jax.shard_map(
        shards,
        mesh=fine,
        in_specs=(
            P(None, seq),
            P(seq, tp),
            P(seq, tp),
            P(seq, tp),
            P(None, seq, tp, None),
            P(None, seq, tp, None),
            P(),
            P(),
            P(tp, seq),
            P(seq),
            P(seq, tp),
            P(seq, tp),
            P(seq, tp),
            P(seq, None, tp, None),
            P(seq, None, tp, None),
            P(seq, None, tp),
        ),
        out_specs=(P(None, seq), P(seq, tp)),
        check_vma=False,
    )
```
